512 devices in a mesh: row: 32 (over y_lo, z), col: 16 (over y_hi, x, core).
Axes of the slice: x: 4, y: 4 (y_hi: 2, y_lo: 2; y = y_hi * 2 + y_lo), z: 16, core: 2. Of those that a mesh axis runs over, the one named last changes fastest.
Arguments:
- image: bfloat16 [32, 2048, 2048], P(None, 'row', 'col'), may hold values from -6 to 6
- weight: bfloat16 [3, 3, 32, 32], replicated, may hold values from -0.375 to 0.375
- bias: float32 [32], replicated, may hold values from -3 to 3
- cotangent: bfloat16 [32, 2048, 2048], P(None, 'row', 'col'), may hold values from -60 to 60
Outputs:
- activation: bfloat16 [32, 2048, 2048], P(None, 'row', 'col')
- grad_image: bfloat16 [32, 2048, 2048], P(None, 'row', 'col')
- grad_weight: float32 [3, 3, 32, 32], replicated
- grad_bias: float32 [32], replicated
The draws below stay inside these ranges and needn't reach their ends.
All inputs are finite; a program needn't handle non-finite values.
Results may differ from the reference program's by a relative error of at most 0.0065.
Values may be sent and summed in bfloat16 or wider, within the bound.
A program may use at most 64 MiB of HBM per device.

```python
import math
import jax
import jax.numpy as jnp
from jax import lax

FEATURE_CHANNELS = 32
DILATION_PIXELS = 16
REGION_HEIGHT = 2048
REGION_WIDTH = 2048


def draw_cotangent(key, part):
    first, second = jax.random.split(jax.random.fold_in(key, 17))
    rows_pos = jnp.arange(REGION_HEIGHT, dtype=jnp.float32) / REGION_HEIGHT
    cols_pos = jnp.arange(REGION_WIDTH, dtype=jnp.float32) / REGION_WIDTH
    noise = jnp.clip(jax.random.normal(first, (FEATURE_CHANNELS, REGION_HEIGHT, REGION_WIDTH), jnp.float32), -6.0, 6.0)
    ramp = 3.0 ** (rows_pos[:, None] + cols_pos[None, :])
    rough = jnp.exp(jax.random.uniform(second, (FEATURE_CHANNELS, REGION_HEIGHT, REGION_WIDTH), jnp.float32, -0.35, 0.35))
    return (noise * ramp[None, :, :] * rough * 0.7).astype(jnp.bfloat16)


def shard_levels(own_key, extent, shards, low, largest):
    factor_of, own = 1.0, jax.random.fold_in(own_key, 6)
    for dim, parts in shards:
        draws = jnp.exp(jax.random.uniform(jax.random.fold_in(own, dim), (parts,), jnp.float32, low / len(shards), largest / len(shards)))
        factor_of = factor_of * jnp.repeat(draws, extent[dim] // parts).reshape([-1 if axis == dim else 1 for axis in range(len(extent))])
    return factor_of


def bell_draw(rng, extent, spread, limit, shards=(), kind=jnp.bfloat16):
    level = shard_levels(rng, extent, shards, -0.22, 0.18) if shards else 1.0
    entries = jax.random.normal(rng, extent, jnp.float32) * spread * level
    return jnp.minimum(jnp.maximum(entries, -limit), limit).astype(kind)


def setup_inputs(seed: int = 0) -> dict:
    streams_of = jax.random.split(jax.random.key(seed), 5)
    image = bell_draw(streams_of[0], (FEATURE_CHANNELS, REGION_HEIGHT, REGION_WIDTH), 1.0, 6.0, ((1, 32), (2, 16)))
    weight = bell_draw(streams_of[1], (3, 3, FEATURE_CHANNELS, FEATURE_CHANNELS), (9 * FEATURE_CHANNELS) ** -0.5, 0.375)
    bias = bell_draw(streams_of[2], (FEATURE_CHANNELS,), 0.5, 3.0, (), jnp.float32)
    cotangent = draw_cotangent(jax.random.fold_in(streams_of[4], 71), 0)
    return {"image": image, "weight": weight, "bias": bias, "cotangent": cotangent}


def gelu_pair(preact):
    coef = 0.7978845608
    cube = preact * preact * preact
    tval = jnp.tanh(coef * (preact + 0.044715 * cube))
    value = 0.5 * preact * (1.0 + tval)
    slope_val = 0.5 * (1.0 + tval) + 0.5 * preact * (1.0 - tval * tval) * coef * (1.0 + 3.0 * 0.044715 * preact * preact)
    return (value, slope_val)

def window(source, row_offset, column_offset):
    start_row = DILATION_PIXELS + row_offset * DILATION_PIXELS
    start_column = DILATION_PIXELS + column_offset * DILATION_PIXELS
    piece = source[:, start_row:start_row + REGION_HEIGHT, start_column:start_column + REGION_WIDTH]
    return piece.reshape(FEATURE_CHANNELS, REGION_HEIGHT * REGION_WIDTH)

def reference(image, weight, bias, cotangent):
    padded_input = jnp.pad(image, ((0, 0), (DILATION_PIXELS, DILATION_PIXELS), (DILATION_PIXELS, DILATION_PIXELS)))
    preact = jnp.zeros((FEATURE_CHANNELS, REGION_HEIGHT * REGION_WIDTH), jnp.float32) + bias.astype(jnp.float32)[:, None]
    for row_offset in (-1, 0, 1):
        for column_offset in (-1, 0, 1):
            preact = preact + jnp.dot(weight[row_offset + 1, column_offset + 1], window(padded_input, row_offset, column_offset), preferred_element_type=jnp.float32)
    value, slope_val = gelu_pair(preact)
    activation = value.astype(jnp.bfloat16).reshape(FEATURE_CHANNELS, REGION_HEIGHT, REGION_WIDTH)
    cot_flat = cotangent.reshape(FEATURE_CHANNELS, REGION_HEIGHT * REGION_WIDTH).astype(jnp.float32)
    preact_gradient = (cot_flat * slope_val).astype(jnp.bfloat16)
    scale = 1.0 / math.sqrt(REGION_HEIGHT * REGION_WIDTH)
    taps = []
    for row_offset in (-1, 0, 1):
        line = []
        for column_offset in (-1, 0, 1):
            line.append(jnp.dot(preact_gradient, window(padded_input, row_offset, column_offset).T, preferred_element_type=jnp.float32) * scale)
        taps.append(jnp.stack(line))
    grad_weight = jnp.stack(taps)
    grad_bias = lax.optimization_barrier(jnp.sum(preact_gradient.astype(jnp.float32), axis=1)) * scale
    padded_gradient = jnp.pad(preact_gradient.reshape(FEATURE_CHANNELS, REGION_HEIGHT, REGION_WIDTH), ((0, 0), (DILATION_PIXELS, DILATION_PIXELS), (DILATION_PIXELS, DILATION_PIXELS)))
    total = jnp.zeros((FEATURE_CHANNELS, REGION_HEIGHT * REGION_WIDTH), jnp.float32)
    for row_offset in (-1, 0, 1):
        for column_offset in (-1, 0, 1):
            total = total + jnp.dot(weight[row_offset + 1, column_offset + 1].T, window(padded_gradient, -row_offset, -column_offset), preferred_element_type=jnp.float32)
    grad_image = total.astype(jnp.bfloat16).reshape(FEATURE_CHANNELS, REGION_HEIGHT, REGION_WIDTH)
    return (activation, grad_image, grad_weight, grad_bias)
```

```python
import math

import jax
import jax.numpy as jnp
from jax import lax
from jax.experimental import pallas as pl
from jax.experimental.pallas import tpu as pltpu
from jax.sharding import PartitionSpec as P

DILATION_PIXELS = 16


def from_behind(value, axis, steps):
    count = lax.axis_size(axis)
    initial, last = (max(0, -steps), min(count, count - steps))
    return lax.ppermute(value, axis, [(source, source + steps) for source in range(initial, last)])


def gelu_pair(preact):
    coef = 0.7978845608
    cube = preact * preact * preact
    tval = jnp.tanh(coef * (preact + 0.044715 * cube))
    value = 0.5 * preact * (1.0 + tval)
    slope_val = 0.5 * (1.0 + tval) + 0.5 * preact * (1.0 - tval * tval) * coef * (
        1.0 + 3.0 * 0.044715 * preact * preact
    )
    return (value, slope_val)


def extended(local_block):
    row_count = local_block.shape[1]
    column_count = local_block.shape[2]
    upper_neighbour = from_behind(local_block[:, row_count - DILATION_PIXELS :, :], "row", 1)
    lower_neighbour = from_behind(local_block[:, :DILATION_PIXELS, :], "row", -1)
    tall_block = jnp.concatenate([upper_neighbour, local_block, lower_neighbour], axis=1)
    left_margin = from_behind(tall_block[:, :, column_count - DILATION_PIXELS :], "col", 1)
    right_margin = from_behind(tall_block[:, :, :DILATION_PIXELS], "col", -1)
    return jnp.concatenate([left_margin, tall_block, right_margin], axis=2)


def tap_view(ext, row_offset, column_offset, row_count, column_count):
    start_row = DILATION_PIXELS + row_offset * DILATION_PIXELS
    start_column = DILATION_PIXELS + column_offset * DILATION_PIXELS
    return ext[:, start_row : start_row + row_count, start_column : start_column + column_count]


def row_stack(ext, row_offset, sign_flip, row_count, column_count):
    return jnp.concatenate(
        [
            tap_view(
                ext, sign_flip * row_offset, sign_flip * column_offset, row_count, column_count
            )
            for column_offset in (-1, 0, 1)
        ],
        axis=0,
    )


MESH = pl.DeviceIdType.MESH
PLANE = 32
DEPTH = 16


def coordinates():
    row = lax.axis_index("row")
    col = lax.axis_index("col")
    z = row % DEPTH
    y = (col // 8) * 2 + row // DEPTH
    x = (col // 2) % 4
    core = col % 2
    return row, col, z, y, x, core


def plane_member(y, x, core, z):
    col = (y // 2) * 8 + x * 2 + core
    row = (y % 2) * DEPTH + z
    return {"row": row, "col": col}, (y % 2) * 16 + col


def plane_offsets():
    far = (2, 1, 3, 0)
    offsets = [(dy, dx, dc) for dy in far for dx in far for dc in (1, 0)]
    offsets = [offset for offset in offsets if offset != (0, 0, 0)]
    hops = lambda d: min(d, 4 - d)
    return sorted(offsets, key=lambda o: -(hops(o[0]) + hops(o[1])))


def plane_peers():
    row, col, z, y, x, core = coordinates()
    peers = []
    for dy, dx, dc in plane_offsets():
        peers.append(plane_member((y + dy) % 4, (x + dx) % 4, (core + dc) % 2, z))
    return peers


def depth_peers():
    row, col, z, y, x, core = coordinates()
    order = sorted(range(1, DEPTH), key=lambda k: -min(k, DEPTH - k))
    return [{"row": (row // DEPTH) * DEPTH + (z + k) % DEPTH, "col": col} for k in order]


def reduce_kernel(terms, total, gathered, layers, piece, send_sem, recv_sem):
    row, col, z, y, x, core = coordinates()
    me = (row // DEPTH) * 16 + col
    plane = plane_peers()
    column = depth_peers()
    barrier = pltpu.get_barrier_semaphore()
    for peer in [p for p, _ in plane] + column:
        pl.semaphore_signal(barrier, inc=1, device_id=peer, device_id_type=MESH)
    pl.semaphore_wait(barrier, len(plane) + len(column))

    def finish(k, buffer):
        copy = pltpu.make_async_copy(buffer, buffer, recv_sem.at[k])
        copy.wait()

    def sent(k, buffer):
        pltpu.make_async_copy(buffer, buffer, send_sem.at[k]).wait()

    for peer, index in plane:
        pltpu.make_async_remote_copy(
            terms.at[index], gathered.at[me], send_sem.at[0], recv_sem.at[0], device_id=peer, device_id_type=MESH
        ).start()
    gathered[me] = terms[me]
    finish(0, gathered.at[pl.ds(0, PLANE - 1)])
    piece[0] = jnp.sum(gathered[...], axis=0)
    for peer in column:
        pltpu.make_async_remote_copy(
            piece.at[0], layers.at[z], send_sem.at[1], recv_sem.at[1], device_id=peer, device_id_type=MESH
        ).start()
    layers[z] = piece[0]
    finish(1, layers.at[pl.ds(0, DEPTH - 1)])
    piece[1] = jnp.sum(layers[...], axis=0)
    for peer, index in plane:
        pltpu.make_async_remote_copy(
            piece.at[1], total.at[me], send_sem.at[2], recv_sem.at[2], device_id=peer, device_id_type=MESH
        ).start()
    total[me] = piece[1]
    finish(2, total.at[pl.ds(0, PLANE - 1)])
    sent(0, gathered.at[pl.ds(0, PLANE - 1)])
    sent(1, layers.at[pl.ds(0, DEPTH - 1)])
    sent(2, total.at[pl.ds(0, PLANE - 1)])


def reduce_all(terms):
    shape = terms.shape
    return pl.pallas_call(
        reduce_kernel,
        out_shape=jax.ShapeDtypeStruct(shape, jnp.float32),
        in_specs=[pl.BlockSpec(memory_space=pltpu.VMEM)],
        out_specs=pl.BlockSpec(memory_space=pltpu.VMEM),
        scratch_shapes=[
            pltpu.VMEM(shape, jnp.float32),
            pltpu.VMEM((DEPTH,) + shape[1:], jnp.float32),
            pltpu.VMEM((2,) + shape[1:], jnp.float32),
            pltpu.SemaphoreType.DMA((3,)),
            pltpu.SemaphoreType.DMA((3,)),
        ],
        compiler_params=pltpu.CompilerParams(collective_id=0, has_side_effects=True),
    )(terms)


def shards(image, weight, bias, cotangent):
    row_count = image.shape[1]
    column_count = image.shape[2]
    channels = image.shape[0]
    height_all = row_count * lax.axis_size("row")
    width_all = column_count * lax.axis_size("col")
    scale = 1.0 / math.sqrt(height_all * width_all)
    image_ext = extended(image)
    preact = jnp.zeros(image.shape, jnp.float32) + bias[:, None, None]
    for row_offset in (-1, 0, 1):
        weight_row = jnp.transpose(weight[row_offset + 1], (1, 0, 2)).reshape(
            channels, 3 * channels
        )
        stacked = row_stack(image_ext, row_offset, 1, row_count, column_count)
        preact = preact + jnp.einsum(
            "ok,krq->orq", weight_row, stacked, preferred_element_type=jnp.float32
        )
    value, slope_val = gelu_pair(preact)
    activation = value.astype(jnp.bfloat16)
    preact_gradient = (cotangent.astype(jnp.float32) * slope_val).astype(jnp.bfloat16)
    taps = []
    for row_offset in (-1, 0, 1):
        stacked = row_stack(image_ext, row_offset, 1, row_count, column_count)
        joined = (
            jnp.einsum("orq,krq->ok", preact_gradient, stacked, preferred_element_type=jnp.float32)
            * scale
        )
        taps.append(joined)
    local_bias = jnp.sum(preact_gradient.astype(jnp.float32), axis=(1, 2)) * scale
    taps[0] = jnp.concatenate([taps[0], local_bias[:, None]], axis=1)
    padded = [jnp.pad(tap, ((0, 0), (0, 128 - tap.shape[1]))) for tap in taps]
    terms = jnp.concatenate(padded, axis=1)[:, None, :]
    total_terms = reduce_all(terms)[:, 0, :]
    grad_bias = total_terms[:, 3 * channels]
    grad_weight = jnp.transpose(
        total_terms.reshape(channels, 3, 128)[:, :, : 3 * channels].reshape(channels, 3, 3, channels),
        (1, 2, 0, 3),
    )
    grad_ext = extended(preact_gradient)
    total = jnp.zeros(image.shape, jnp.float32)
    for row_offset in (-1, 0, 1):
        weight_row = weight[row_offset + 1].reshape(3 * channels, channels)
        stacked = row_stack(grad_ext, row_offset, -1, row_count, column_count)
        total = total + jnp.einsum(
            "kc,krq->crq", weight_row, stacked, preferred_element_type=jnp.float32
        )
    grad_image = total.astype(jnp.bfloat16)
    return (activation, grad_image, grad_weight, grad_bias)


def solution(mesh):
    return jax.shard_map(
        shards,
        mesh=mesh,
        in_specs=(P(None, "row", "col"), P(), P(), P(None, "row", "col")),
        out_specs=(P(None, "row", "col"), P(None, "row", "col"), P(), P()),
        check_vma=False,
    )
```

```python
import math

import jax
import jax.numpy as jnp
from jax import lax
from jax.experimental import pallas as pl
from jax.experimental.pallas import tpu as pltpu
from jax.sharding import PartitionSpec as P

MESH = pl.DeviceIdType.MESH
BF16 = jnp.bfloat16
F32 = jnp.float32
DIL = 16
LANES = 128
PLANE = 32
DEPTH = 16
COEF = 0.7978845608
CUBIC = 0.044715


def ring_order(count):
    return sorted(range(1, count), key=lambda k: -min(k, count - k))


def gelu_pair(z):
    square = z * z
    t = jnp.tanh(z * (COEF + (COEF * CUBIC) * square))
    half = 0.5 + 0.5 * t
    bend = (1.0 - t * t) * (0.5 * COEF + (1.5 * COEF * CUBIC) * square)
    return z * half, half + z * bend


def lanes_of(row, count=1):
    return slice(row * LANES, (row + count) * LANES)


def body(
    rows, scale,
    image, weight, bias, cotangent,
    act_out, grad_out, gw_out, gb_out,
    xin, cin, cot, stack, gstack, xleft, xright, gleft, gright,
    pack_l, pack_r, act, act_c, grad_c, accs,
    terms, gathered, layers, piece, total,
    local_sem, xsend, xrecv, gsend, grecv, rsend, rrecv, chain_a, chain_b,
):
    channels = image.shape[0]
    ext = rows + 2 * DIL
    groups = rows // 8
    row = lax.axis_index("row")
    col = lax.axis_index("col")
    nrow, ncol = lax.axis_size("row"), lax.axis_size("col")
    z = row % DEPTH
    y = (col // 8) * 2 + row // DEPTH
    x = (col // 2) % 4
    core = col % 2
    me = (row // DEPTH) * 16 + col

    def at(drow, dcol):
        return {"row": (row + drow + nrow) % nrow, "col": (col + dcol + ncol) % ncol}

    def deep(k):
        return {"row": (row // DEPTH) * DEPTH + (z + k + DEPTH) % DEPTH, "col": col}

    hops = lambda d: min(d, 4 - d)
    offsets = [(dy, dx, dc) for dy in range(4) for dx in range(4) for dc in range(2)][1:]
    offsets = sorted(offsets, key=lambda o: -(hops(o[0]) + hops(o[1])))
    plane = []
    for dy, dx, dc in offsets:
        py, px, pc = (y + dy) % 4, (x + dx) % 4, (core + dc) % 2
        pcol = (py // 2) * 8 + px * 2 + pc
        plane.append(({"row": (py % 2) * DEPTH + z, "col": pcol}, (py % 2) * 16 + pcol))

    barrier = pltpu.get_barrier_semaphore()
    near = [at(-1, 0), at(1, 0), at(-1, -1), at(-1, 1), at(1, -1), at(1, 1)]
    near += [deep(k) for k in (3, -3, 2, -2, 1, -1)]
    greeted = near + [peer for peer, _ in plane]
    for peer in greeted:
        pl.semaphore_signal(barrier, inc=1, device_id=peer, device_id_type=MESH)

    load_x = pltpu.make_async_copy(image, xin.at[:, DIL : DIL + rows, :], local_sem.at[0])
    load_c = pltpu.make_async_copy(cotangent, cin, local_sem.at[1])
    load_x.start()
    load_c.start()

    lane = lax.broadcasted_iota(jnp.int32, (channels, LANES), 1)
    slot = lane // DIL
    forward = [
        jnp.concatenate([weight[a, e] for e in range(3)], axis=1) for a in range(3)
    ]
    backward = [
        jnp.concatenate([weight[2 - a, 2 - e].T for e in range(3)], axis=1) for a in range(3)
    ]
    sub = lax.broadcasted_iota(jnp.int32, (channels, channels), 0)
    lan = lax.broadcasted_iota(jnp.int32, (channels, channels), 1)
    offset = jnp.sum(jnp.where(sub == lan, bias[...], 0.0), axis=1, keepdims=True)
    accs[...] = jnp.zeros_like(accs)

    top, bottom = row == 0, row == nrow - 1
    first, last = col == 0, col == ncol - 1
    has = {
        "u": row > 0, "d": row < nrow - 1, "l": col > 0, "r": col < ncol - 1,
        "ul": (row > 0) & (col > 0), "ur": (row > 0) & (col < ncol - 1),
        "dl": (row < nrow - 1) & (col > 0), "dr": (row < nrow - 1) & (col < ncol - 1),
    }
    step = {
        "u": (-1, 0), "d": (1, 0), "l": (0, -1), "r": (0, 1),
        "ul": (-1, -1), "ur": (-1, 1), "dl": (1, -1), "dr": (1, 1),
    }
    mirror = {"u": "d", "d": "u", "l": "r", "r": "l", "ul": "dr", "dr": "ul", "ur": "dl", "dl": "ur"}
    names = list(step)

    def halo_copies(top_src, bottom_src, top_dst, bottom_dst, left, right, send, recv):
        src_dst = {
            "u": (top_src, bottom_dst),
            "d": (bottom_src, top_dst),
            "l": (pack_l, right.at[2 : 2 + groups]),
            "r": (pack_r, left.at[2 : 2 + groups]),
            "ul": (pack_l.at[0:2], right.at[2 + groups : 4 + groups]),
            "ur": (pack_r.at[0:2], left.at[2 + groups : 4 + groups]),
            "dl": (pack_l.at[groups - 2 : groups], right.at[0:2]),
            "dr": (pack_r.at[groups - 2 : groups], left.at[0:2]),
        }
        return {
            n: pltpu.make_async_remote_copy(
                src, dst, send.at[names.index(n)], recv.at[names.index(n)],
                device_id=at(*step[n]), device_id_type=MESH,
            )
            for n, (src, dst) in src_dst.items()
        }

    def when_each(directions, predicate, action):
        for n in directions:
            pl.when(predicate(n))(lambda n=n: action(n))

    def send(copies, directions):
        when_each(directions, lambda n: has[n], lambda n: copies[n].start())

    def await_from(copies, directions):
        when_each(directions, lambda n: has[n], lambda n: copies[mirror[n]].wait_recv())

    def await_sent(copies):
        when_each(names, lambda n: has[n], lambda n: copies[n].wait_send())

    def zero_edges(left, right, top_dst, bottom_dst):
        pl.when(first)(lambda: left.__setitem__(Ellipsis, jnp.zeros_like(left)))
        pl.when(last)(lambda: right.__setitem__(Ellipsis, jnp.zeros_like(right)))

        @pl.when(top)
        def _():
            top_dst[...] = jnp.zeros(top_dst.shape, BF16)
            left[0:2] = jnp.zeros((2,) + left.shape[1:], BF16)
            right[0:2] = jnp.zeros((2,) + left.shape[1:], BF16)

        @pl.when(bottom)
        def _():
            bottom_dst[...] = jnp.zeros(bottom_dst.shape, BF16)
            left[2 + groups : 4 + groups] = jnp.zeros((2,) + left.shape[1:], BF16)
            right[2 + groups : 4 + groups] = jnp.zeros((2,) + left.shape[1:], BF16)

    def pack(source, g):
        lefts, rights = None, None
        for k in range(8):
            v = source[channels : 2 * channels, lanes_of(DIL + 8 * g + k)]
            a = v if k == 0 else pltpu.roll(v, DIL * k, 1)
            b = v if k == 7 else pltpu.roll(v, DIL * k + DIL, 1)
            lefts = a if k == 0 else jnp.where(slot == k, a, lefts)
            rights = b if k == 0 else jnp.where(slot == k, b, rights)
        pack_l[g] = lefts
        pack_r[g] = rights

    def shift_row(source, r):
        v = source[channels : 2 * channels, lanes_of(r)]
        source[0:channels, lanes_of(r)] = pltpu.roll(v, DIL, 1)
        source[2 * channels : 3 * channels, lanes_of(r)] = pltpu.roll(v, LANES - DIL, 1)

    def merge_group(source, left, right, g):
        lv, rv = left[g], right[g]
        for k in range(8):
            r = lanes_of(8 * g + k)
            a = lv if k == 0 else pltpu.roll(lv, LANES - DIL * k, 1)
            b = rv if k == 7 else pltpu.roll(rv, LANES - DIL - DIL * k, 1)
            source[0:channels, r] = jnp.where(lane < DIL, a, source[0:channels, r])
            source[2 * channels : 3 * channels, r] = jnp.where(
                lane >= LANES - DIL, b, source[2 * channels : 3 * channels, r]
            )

    def transpose_in(src, src_row, dst, part, dst_row):
        v = jnp.transpose(src[:, src_row : src_row + DIL, :], (1, 0, 2))
        for h in range(DIL):
            dst[part : part + channels, lanes_of(dst_row + h)] = v[h]

    def transpose_out(value, dst, dst_row):
        v = jnp.stack([value[:, lanes_of(h)] for h in range(DIL)], axis=0)
        dst[:, dst_row : dst_row + DIL, :] = jnp.transpose(v, (1, 0, 2))

    center = slice(channels, 2 * channels)
    bias_sum = [jnp.zeros((channels, LANES), F32)]

    def forward_rows(r0, count):
        for r in range(r0, r0 + count, 8):
            z_val = offset
            for a in range(3):
                z_val = z_val + jnp.dot(
                    forward[a], stack[:, lanes_of(r + DIL * a, 8)], preferred_element_type=F32
                )
            value, slope = gelu_pair(z_val)
            act[:, lanes_of(r, 8)] = value.astype(BF16)
            g = (cot[:, lanes_of(r, 8)].astype(F32) * slope).astype(BF16)
            gstack[center, lanes_of(r + DIL, 8)] = g
            wide = g.astype(F32)
            part = bias_sum[0]
            for h in range(8):
                part = part + wide[:, lanes_of(h)]
            bias_sum[0] = part

    def weight_term(a, h0, count):
        return lax.dot_general(
            gstack[center, lanes_of(DIL + h0, count)],
            stack[:, lanes_of(h0 + DIL * a, count)],
            (((1,), (1,)), ((), ())),
            preferred_element_type=F32,
        )

    load_x.wait()
    for h in range(0, rows, DIL):
        transpose_in(xin, DIL + h, stack, channels, DIL + h)
    for g in range(groups):
        pack(stack, g)
    pl.semaphore_wait(barrier, len(greeted))

    xcopies = halo_copies(
        xin.at[:, DIL : 2 * DIL, :], xin.at[:, rows : rows + DIL, :],
        xin.at[:, 0:DIL, :], xin.at[:, rows + DIL : ext, :],
        xleft, xright, xsend, xrecv,
    )
    send(xcopies, ["u", "d", "l", "r", "ul", "ur", "dl", "dr"])
    for k in (3, -3):
        pl.semaphore_signal(chain_a, inc=1, device_id=deep(k), device_id_type=MESH)

    zero_edges(xleft, xright, xin.at[:, 0:DIL, :], xin.at[:, rows + DIL : ext, :])
    for h in range(rows):
        shift_row(stack, DIL + h)
    load_c.wait()
    for h in range(0, rows, DIL):
        transpose_in(cin, h, cot, 0, h)

    await_from(xcopies, ["l", "r"])
    for g in range(2, 2 + groups):
        merge_group(stack, xleft, xright, g)
    forward_rows(DIL, rows - 2 * DIL)
    inner = [weight_term(a, DIL, rows - 2 * DIL) for a in range(3)]
    for a in range(3):
        accs[a, :, 0 : 3 * channels] = inner[a]
    pl.semaphore_wait(chain_a, 2)
    for k in (2, -2):
        pl.semaphore_signal(chain_b, inc=1, device_id=deep(k), device_id_type=MESH)

    await_from(xcopies, ["u", "d", "ul", "ur", "dl", "dr"])
    for base, g0 in ((0, 0), (rows + DIL, 2 + groups)):
        transpose_in(xin, base, stack, channels, base)
        for h in range(DIL):
            shift_row(stack, base + h)
        for g in (g0, g0 + 1):
            merge_group(stack, xleft, xright, g)
    forward_rows(0, DIL)
    forward_rows(rows - DIL, DIL)
    await_sent(xcopies)
    for g in range(groups):
        pack(gstack, g)
    gcopies = halo_copies(
        gstack.at[center, lanes_of(DIL, DIL)], gstack.at[center, lanes_of(rows, DIL)],
        gstack.at[center, lanes_of(0, DIL)], gstack.at[center, lanes_of(rows + DIL, DIL)],
        gleft, gright, gsend, grecv,
    )
    send(gcopies, ["u", "d", "l", "r", "ul", "ur", "dl", "dr"])
    for a in range(3):
        accs[a, :, 0 : 3 * channels] += weight_term(a, 0, DIL) + weight_term(a, rows - DIL, DIL)
    accs[0, :, 3 * channels : 3 * channels + 1] = jnp.sum(bias_sum[0], axis=1, keepdims=True)
    for a in range(3):
        terms[:, 0, lanes_of(a)] = accs[a]

    def remote(src, dst, k, peer):
        pltpu.make_async_remote_copy(
            src, dst, rsend.at[k], rrecv.at[k], device_id=peer, device_id_type=MESH
        ).start()

    def drain(sem, buffer):
        pltpu.make_async_copy(buffer, buffer, sem).wait()

    for peer, index in plane:
        remote(terms.at[index], gathered.at[me], 0, peer)
    gathered[me] = terms[me]

    for h in range(0, rows, DIL):
        transpose_out(act[:, lanes_of(h, DIL)], act_c, h)
    store_a = pltpu.make_async_copy(act_c, act_out, local_sem.at[2])
    store_a.start()
    zero_edges(
        gleft, gright,
        gstack.at[center, lanes_of(0, DIL)], gstack.at[center, lanes_of(rows + DIL, DIL)],
    )
    for h in range(rows):
        shift_row(gstack, DIL + h)
    pl.semaphore_wait(chain_b, 2)

    drain(rrecv.at[0], gathered.at[pl.ds(0, PLANE - 1)])
    piece[0] = jnp.sum(gathered[...], axis=0)
    for k in ring_order(DEPTH):
        remote(piece.at[0], layers.at[z], 1, deep(k))
    layers[z] = piece[0]

    await_from(gcopies, names)
    for base in (0, rows + DIL):
        for h in range(DIL):
            shift_row(gstack, base + h)
    for g in range(4 + groups):
        merge_group(gstack, gleft, gright, g)
    for h in range(0, rows, DIL):
        tiles = []
        for r in (h, h + 8):
            out = None
            for a in range(3):
                d = jnp.dot(
                    backward[a], gstack[:, lanes_of(r + DIL * a, 8)], preferred_element_type=F32
                )
                out = d if out is None else out + d
            tiles.append(out.astype(BF16))
        transpose_out(jnp.concatenate(tiles, axis=1), grad_c, h)
    store_g = pltpu.make_async_copy(grad_c, grad_out, local_sem.at[3])
    store_g.start()

    drain(rrecv.at[1], layers.at[pl.ds(0, DEPTH - 1)])
    piece[1] = jnp.sum(layers[...], axis=0) * scale
    for peer, index in plane:
        remote(piece.at[1], total.at[me], 2, peer)
    total[me] = piece[1]
    await_sent(gcopies)
    store_a.wait()
    store_g.wait()
    drain(rsend.at[0], gathered.at[pl.ds(0, PLANE - 1)])
    drain(rsend.at[1], layers.at[pl.ds(0, DEPTH - 1)])
    drain(rrecv.at[2], total.at[pl.ds(0, PLANE - 1)])
    for a in range(3):
        tile = total[:, 0, lanes_of(a)]
        for e in range(3):
            gw_out[a, e] = tile[:, e * channels : (e + 1) * channels]
        if a == 0:
            column = tile[:, 3 * channels : 3 * channels + 1]
            gb_out[...] = jnp.sum(jnp.where(sub == lan, column, 0.0), axis=0, keepdims=True)
    drain(rsend.at[2], total.at[pl.ds(0, PLANE - 1)])


def shards(image, weight, bias, cotangent):
    channels, rows, columns = image.shape
    assert columns == LANES and rows % DIL == 0 and channels == PLANE
    count = rows * lax.axis_size("row") * columns * lax.axis_size("col")
    scale = 1.0 / math.sqrt(count)
    ext = rows + 2 * DIL
    groups = rows // 8
    vmem = pl.BlockSpec(memory_space=pltpu.VMEM)
    hbm = pl.BlockSpec(memory_space=pl.ANY)
    rim = pltpu.VMEM((groups + 4, channels, LANES), BF16)
    edge = pltpu.VMEM((groups, channels, LANES), BF16)
    tile = pltpu.VMEM((channels, rows, LANES), BF16)
    line = (1, 3 * LANES)

    def kernel(*refs):
        body(rows, scale, *refs)

    act, grad, gw, gb = pl.pallas_call(
        kernel,
        out_shape=(
            jax.ShapeDtypeStruct(image.shape, BF16),
            jax.ShapeDtypeStruct(image.shape, BF16),
            jax.ShapeDtypeStruct(weight.shape, F32),
            jax.ShapeDtypeStruct((1, channels), F32),
        ),
        in_specs=[hbm, vmem, vmem, hbm],
        out_specs=(hbm, hbm, vmem, vmem),
        scratch_shapes=[
            pltpu.VMEM((channels, ext, LANES), BF16),
            tile,
            pltpu.VMEM((channels, rows * LANES), BF16),
            pltpu.VMEM((3 * channels, ext * LANES), BF16),
            pltpu.VMEM((3 * channels, ext * LANES), BF16),
            rim, rim, rim, rim, edge, edge,
            pltpu.VMEM((channels, rows * LANES), BF16),
            tile, tile,
            pltpu.VMEM((3, channels, LANES), F32),
            pltpu.VMEM((PLANE,) + line, F32),
            pltpu.VMEM((PLANE,) + line, F32),
            pltpu.VMEM((DEPTH,) + line, F32),
            pltpu.VMEM((2,) + line, F32),
            pltpu.VMEM((PLANE,) + line, F32),
            pltpu.SemaphoreType.DMA((4,)),
            pltpu.SemaphoreType.DMA((8,)),
            pltpu.SemaphoreType.DMA((8,)),
            pltpu.SemaphoreType.DMA((8,)),
            pltpu.SemaphoreType.DMA((8,)),
            pltpu.SemaphoreType.DMA((3,)),
            pltpu.SemaphoreType.DMA((3,)),
            pltpu.SemaphoreType.REGULAR,
            pltpu.SemaphoreType.REGULAR,
        ],
        compiler_params=pltpu.CompilerParams(collective_id=0, has_side_effects=True),
    )(image, weight, bias.reshape(1, channels), cotangent)
    return act, grad, gw, gb.reshape(channels)


def solution(mesh):
    return jax.shard_map(
        shards,
        mesh=mesh,
        in_specs=(P(None, "row", "col"), P(), P(), P(None, "row", "col")),
        out_specs=(P(None, "row", "col"), P(None, "row", "col"), P(), P()),
        check_vma=False,
    )
```

```python
import math

import jax
import jax.numpy as jnp
from jax import lax
from jax.experimental import pallas as pl
from jax.experimental.pallas import tpu as pltpu
from jax.sharding import PartitionSpec as P

MESH = pl.DeviceIdType.MESH
BF16 = jnp.bfloat16
F32 = jnp.float32
DIL = 16
LANES = 128
PLANE = 32
DEPTH = 16
COEF = 0.7978845608
CUBIC = 0.044715


def ring_order(count):
    return sorted(range(1, count), key=lambda k: -min(k, count - k))


def gelu_pair(z):
    square = z * z
    t = jnp.tanh(z * (COEF + (COEF * CUBIC) * square))
    half = 0.5 + 0.5 * t
    bend = (1.0 - t * t) * (0.5 * COEF + (1.5 * COEF * CUBIC) * square)
    return z * half, half + z * bend


def lanes_of(row, count=1):
    return slice(row * LANES, (row + count) * LANES)


def body(
    rows, scale,
    image, weight_in, bias_in, cotangent,
    act_c, grad_c, total,
    weight, bias, xin, cin, cot, stack, gstack, xleft, xright, gleft, gright,
    pack_l, pack_r, act, accs,
    terms, gathered, layers, piece,
    local_sem, xsend, xrecv, gsend, grecv, rsend, rrecv, chain_a, chain_b,
):
    channels = image.shape[0]
    ext = rows + 2 * DIL
    groups = rows // 8
    row = lax.axis_index("row")
    col = lax.axis_index("col")
    nrow, ncol = lax.axis_size("row"), lax.axis_size("col")
    z = row % DEPTH
    y = (col // 8) * 2 + row // DEPTH
    x = (col // 2) % 4
    core = col % 2
    me = (row // DEPTH) * 16 + col

    def at(drow, dcol):
        return {"row": (row + drow + nrow) % nrow, "col": (col + dcol + ncol) % ncol}

    def deep(k):
        return {"row": (row // DEPTH) * DEPTH + (z + k + DEPTH) % DEPTH, "col": col}

    hops = lambda d: min(d, 4 - d)
    offsets = [(dy, dx, dc) for dy in range(4) for dx in range(4) for dc in range(2)][1:]
    offsets = sorted(offsets, key=lambda o: -(hops(o[0]) + hops(o[1])))
    plane = []
    for dy, dx, dc in offsets:
        py, px, pc = (y + dy) % 4, (x + dx) % 4, (core + dc) % 2
        pcol = (py // 2) * 8 + px * 2 + pc
        plane.append(({"row": (py % 2) * DEPTH + z, "col": pcol}, (py % 2) * 16 + pcol))

    barrier = pltpu.get_barrier_semaphore()
    greeted = [at(-1, 0), at(1, 0), at(0, -1), at(0, 1), at(-1, -1), at(-1, 1), at(1, -1), at(1, 1)]
    greeted += [deep(k) for k in (2, -2, 1, -1)]
    greeted += [peer for (peer, _), o in zip(plane, offsets) if hops(o[0]) + hops(o[1]) <= 2]
    for peer in greeted:
        pl.semaphore_signal(barrier, inc=1, device_id=peer, device_id_type=MESH)

    load_x = pltpu.make_async_copy(image, xin.at[:, DIL : DIL + rows, :], local_sem.at[0])
    load_c = pltpu.make_async_copy(cotangent, cin, local_sem.at[1])
    load_w = pltpu.make_async_copy(weight_in, weight, local_sem.at[2])
    load_b = pltpu.make_async_copy(bias_in, bias, local_sem.at[3])
    for load in (load_x, load_w, load_b, load_c):
        load.start()

    lane = lax.broadcasted_iota(jnp.int32, (channels, LANES), 1)
    slot = lane // DIL
    top, bottom = row == 0, row == nrow - 1
    first, last = col == 0, col == ncol - 1
    has = {
        "u": row > 0, "d": row < nrow - 1, "l": col > 0, "r": col < ncol - 1,
        "ul": (row > 0) & (col > 0), "ur": (row > 0) & (col < ncol - 1),
        "dl": (row < nrow - 1) & (col > 0), "dr": (row < nrow - 1) & (col < ncol - 1),
    }
    step = {
        "u0": (-1, 0), "d0": (1, 0), "u1": (-1, 0), "d1": (1, 0), "l": (0, -1), "r": (0, 1),
        "ul": (-1, -1), "ur": (-1, 1), "dl": (1, -1), "dr": (1, 1),
    }
    mirror = {
        "u0": "d0", "d0": "u0", "u1": "d1", "d1": "u1", "l": "r", "r": "l",
        "ul": "dr", "dr": "ul", "ur": "dl", "dl": "ur",
    }
    for n in ("u0", "u1", "d0", "d1"):
        has[n] = has[n[0]]
    names = list(step)
    vertical = ["d0", "u0", "d1", "u1"]
    sideways = ["l", "r", "ul", "ur", "dl", "dr"]

    def halo_copies(top_src, bottom_src, top_dst, bottom_dst, left, right, send, recv):
        src_dst = {
            "u0": (top_src(0), bottom_dst(0)),
            "u1": (top_src(1), bottom_dst(1)),
            "d0": (bottom_src(0), top_dst(0)),
            "d1": (bottom_src(1), top_dst(1)),
            "l": (pack_l, right.at[2 : 2 + groups]),
            "r": (pack_r, left.at[2 : 2 + groups]),
            "ul": (pack_l.at[0:2], right.at[2 + groups : 4 + groups]),
            "ur": (pack_r.at[0:2], left.at[2 + groups : 4 + groups]),
            "dl": (pack_l.at[groups - 2 : groups], right.at[0:2]),
            "dr": (pack_r.at[groups - 2 : groups], left.at[0:2]),
        }
        return {
            n: pltpu.make_async_remote_copy(
                src, dst, send.at[names.index(n)], recv.at[names.index(n)],
                device_id=at(*step[n]), device_id_type=MESH,
            )
            for n, (src, dst) in src_dst.items()
        }

    def when_each(directions, predicate, action):
        for n in directions:
            pl.when(predicate(n))(lambda n=n: action(n))

    def send(copies, directions):
        when_each(directions, lambda n: has[n], lambda n: copies[n].start())

    def await_from(copies, directions):
        when_each(directions, lambda n: has[n], lambda n: copies[mirror[n]].wait_recv())

    def await_sent(copies):
        when_each(names, lambda n: has[n], lambda n: copies[n].wait_send())

    def zero_edges(left, right, top_dst, bottom_dst):
        pl.when(first)(lambda: left.__setitem__(Ellipsis, jnp.zeros_like(left)))
        pl.when(last)(lambda: right.__setitem__(Ellipsis, jnp.zeros_like(right)))

        @pl.when(top)
        def _():
            top_dst[...] = jnp.zeros(top_dst.shape, BF16)
            left[0:2] = jnp.zeros((2,) + left.shape[1:], BF16)
            right[0:2] = jnp.zeros((2,) + left.shape[1:], BF16)

        @pl.when(bottom)
        def _():
            bottom_dst[...] = jnp.zeros(bottom_dst.shape, BF16)
            left[2 + groups : 4 + groups] = jnp.zeros((2,) + left.shape[1:], BF16)
            right[2 + groups : 4 + groups] = jnp.zeros((2,) + left.shape[1:], BF16)

    def pack(source, g):
        lefts, rights = None, None
        for k in range(8):
            v = source[channels : 2 * channels, lanes_of(DIL + 8 * g + k)]
            a = v if k == 0 else pltpu.roll(v, DIL * k, 1)
            b = v if k == 7 else pltpu.roll(v, DIL * k + DIL, 1)
            lefts = a if k == 0 else jnp.where(slot == k, a, lefts)
            rights = b if k == 0 else jnp.where(slot == k, b, rights)
        pack_l[g] = lefts
        pack_r[g] = rights

    def shift_row(source, r):
        v = source[channels : 2 * channels, lanes_of(r)]
        source[0:channels, lanes_of(r)] = pltpu.roll(v, DIL, 1)
        source[2 * channels : 3 * channels, lanes_of(r)] = pltpu.roll(v, LANES - DIL, 1)

    def merge_group(source, left, right, g):
        lv, rv = left[g], right[g]
        for k in range(8):
            r = lanes_of(8 * g + k)
            a = lv if k == 0 else pltpu.roll(lv, LANES - DIL * k, 1)
            b = rv if k == 7 else pltpu.roll(rv, LANES - DIL - DIL * k, 1)
            source[0:channels, r] = jnp.where(lane < DIL, a, source[0:channels, r])
            source[2 * channels : 3 * channels, r] = jnp.where(
                lane >= LANES - DIL, b, source[2 * channels : 3 * channels, r]
            )

    def transpose_in(src, src_row, dst, part, dst_row, count=DIL):
        v = jnp.transpose(src[:, src_row : src_row + count, :], (1, 0, 2))
        for h in range(count):
            dst[part : part + channels, lanes_of(dst_row + h)] = v[h]

    def transpose_out(value, dst, dst_row):
        v = jnp.stack([value[:, lanes_of(h)] for h in range(DIL)], axis=0)
        dst[:, dst_row : dst_row + DIL, :] = jnp.transpose(v, (1, 0, 2))

    center = slice(channels, 2 * channels)
    bias_sum = [jnp.zeros((channels, LANES), F32)]

    def forward_rows(r0, count):
        for r in range(r0, r0 + count, 8):
            z_val = offset
            for a in range(3):
                z_val = z_val + jnp.dot(
                    forward[a], stack[:, lanes_of(r + DIL * a, 8)], preferred_element_type=F32
                )
            value, slope = gelu_pair(z_val)
            act[:, lanes_of(r, 8)] = value.astype(BF16)
            g = (cot[:, lanes_of(r, 8)].astype(F32) * slope).astype(BF16)
            gstack[center, lanes_of(r + DIL, 8)] = g
            wide = g.astype(F32)
            part = bias_sum[0]
            for h in range(8):
                part = part + wide[:, lanes_of(h)]
            bias_sum[0] = part

    def weight_term(a, h0, count):
        return lax.dot_general(
            gstack[center, lanes_of(DIL + h0, count)],
            stack[:, lanes_of(h0 + DIL * a, count)],
            (((1,), (1,)), ((), ())),
            preferred_element_type=F32,
        )

    def rows_of(ref, r0):
        return lambda k: ref.at[:, r0 + 8 * k : r0 + 8 * k + 8, :]

    def lines_of(r0):
        return lambda k: gstack.at[center, lanes_of(r0 + 8 * k, 8)]

    pl.semaphore_wait(barrier, len(greeted))
    xcopies = halo_copies(
        rows_of(image, 0), rows_of(image, rows - DIL), rows_of(xin, 0), rows_of(xin, rows + DIL),
        xleft, xright, xsend, xrecv,
    )
    send(xcopies, vertical)

    load_x.wait()
    for h in range(0, rows, DIL):
        transpose_in(xin, DIL + h, stack, channels, DIL + h)
    for g in range(groups):
        pack(stack, g)
    send(xcopies, sideways)
    chain = [peer for (peer, _), o in zip(plane, offsets) if o[0] % 2 and o[1] % 2 and o[2] == 0]
    chain += [deep(2), deep(-2)]
    for peer in chain:
        pl.semaphore_signal(chain_a, inc=1, device_id=peer, device_id_type=MESH)

    zero_edges(xleft, xright, xin.at[:, 0:DIL, :], xin.at[:, rows + DIL : ext, :])
    for h in range(rows):
        shift_row(stack, DIL + h)
    load_c.wait()
    for h in range(0, rows, DIL):
        transpose_in(cin, h, cot, 0, h)
    load_w.wait()
    load_b.wait()
    forward = [
        jnp.concatenate([weight[a, e] for e in range(3)], axis=1) for a in range(3)
    ]
    backward = [
        jnp.concatenate([weight[2 - a, 2 - e].T for e in range(3)], axis=1) for a in range(3)
    ]
    sub = lax.broadcasted_iota(jnp.int32, (channels, channels), 0)
    lan = lax.broadcasted_iota(jnp.int32, (channels, channels), 1)
    offset = jnp.sum(jnp.where(sub == lan, bias[...], 0.0), axis=1, keepdims=True)
    accs[...] = jnp.zeros_like(accs)


    await_from(xcopies, ["l", "r"])
    for g in range(2, 2 + groups):
        merge_group(stack, xleft, xright, g)
    forward_rows(DIL, rows - 2 * DIL)
    inner = [weight_term(a, DIL, rows - 2 * DIL) for a in range(3)]

    for k in range(2):
        await_from(xcopies, [f"u{k}", f"d{k}"] + (["ul", "ur", "dl", "dr"] if k == 0 else []))
        for base, g in ((8 * k, k), (rows + DIL + 8 * k, 2 + groups + k)):
            transpose_in(xin, base, stack, channels, base, 8)
            for h in range(8):
                shift_row(stack, base + h)
            merge_group(stack, xleft, xright, g)
        for r in (8 * k, rows - DIL + 8 * k):
            forward_rows(r, 8)
            for a in range(3):
                inner[a] = inner[a] + weight_term(a, r, 8)
    for a in range(3):
        accs[a, :, 0 : 3 * channels] = inner[a]
    accs[0, :, 3 * channels : 3 * channels + 1] = jnp.sum(bias_sum[0], axis=1, keepdims=True)
    for a in range(3):
        terms[:, 0, lanes_of(a)] = accs[a]
    pl.semaphore_wait(chain_a, len(chain))
    for k in (4, -4):
        pl.semaphore_signal(chain_b, inc=1, device_id=deep(k), device_id_type=MESH)

    def remote(src, dst, k, peer):
        pltpu.make_async_remote_copy(
            src, dst, rsend.at[k], rrecv.at[k], device_id=peer, device_id_type=MESH
        ).start()

    def drain(sem, buffer):
        pltpu.make_async_copy(buffer, buffer, sem).wait()

    for peer, index in plane:
        remote(terms.at[index], gathered.at[me], 0, peer)
    gathered[me] = terms[me]

    await_sent(xcopies)
    gcopies = halo_copies(
        lines_of(DIL), lines_of(rows), lines_of(0), lines_of(rows + DIL), gleft, gright, gsend, grecv,
    )
    send(gcopies, vertical)
    for g in range(groups):
        pack(gstack, g)
    send(gcopies, sideways)
    zero_edges(
        gleft, gright,
        gstack.at[center, lanes_of(0, DIL)], gstack.at[center, lanes_of(rows + DIL, DIL)],
    )
    for h in range(0, rows, DIL):
        transpose_out(act[:, lanes_of(h, DIL)], act_c, h)
    for h in range(rows):
        shift_row(gstack, DIL + h)
    pl.semaphore_wait(chain_b, 2)

    drain(rrecv.at[0], gathered.at[pl.ds(0, PLANE - 1)])
    piece[0] = jnp.sum(gathered[...], axis=0)
    for k in ring_order(DEPTH):
        remote(piece.at[0], layers.at[z], 1, deep(k))
    layers[z] = piece[0]

    await_from(gcopies, names)
    for base in (0, rows + DIL):
        for h in range(DIL):
            shift_row(gstack, base + h)
    for g in range(4 + groups):
        merge_group(gstack, gleft, gright, g)
    for h in range(0, rows, DIL):
        tiles = []
        for r in (h, h + 8):
            out = None
            for a in range(3):
                d = jnp.dot(
                    backward[a], gstack[:, lanes_of(r + DIL * a, 8)], preferred_element_type=F32
                )
                out = d if out is None else out + d
            tiles.append(out.astype(BF16))
        transpose_out(jnp.concatenate(tiles, axis=1), grad_c, h)

    drain(rrecv.at[1], layers.at[pl.ds(0, DEPTH - 1)])
    piece[1] = jnp.sum(layers[...], axis=0) * scale
    for peer, index in plane:
        remote(piece.at[1], total.at[me], 2, peer)
    total[me] = piece[1]
    await_sent(gcopies)
    drain(rsend.at[0], gathered.at[pl.ds(0, PLANE - 1)])
    drain(rsend.at[1], layers.at[pl.ds(0, DEPTH - 1)])
    drain(rrecv.at[2], total.at[pl.ds(0, PLANE - 1)])
    drain(rsend.at[2], total.at[pl.ds(0, PLANE - 1)])


def write_out(act_c, grad_c, total, act_out, grad_out, gw_out, gb_out, sem):
    channels = act_c.shape[0]
    copies = [
        pltpu.make_async_copy(act_c, act_out, sem.at[0]),
        pltpu.make_async_copy(grad_c, grad_out, sem.at[1]),
    ]
    for copy in copies:
        copy.start()
    sub = lax.broadcasted_iota(jnp.int32, (channels, channels), 0)
    lan = lax.broadcasted_iota(jnp.int32, (channels, channels), 1)
    for a in range(3):
        tile = total[:, 0, lanes_of(a)]
        for e in range(3):
            gw_out[a, e] = tile[:, e * channels : (e + 1) * channels]
        if a == 0:
            column = tile[:, 3 * channels : 3 * channels + 1]
            gb_out[...] = jnp.sum(jnp.where(sub == lan, column, 0.0), axis=0, keepdims=True)
    for copy in copies:
        copy.wait()


def shards(image, weight, bias, cotangent):
    channels, rows, columns = image.shape
    assert columns == LANES and rows % DIL == 0 and channels == PLANE
    count = rows * lax.axis_size("row") * columns * lax.axis_size("col")
    scale = 1.0 / math.sqrt(count)
    ext = rows + 2 * DIL
    groups = rows // 8
    vmem = pl.BlockSpec(memory_space=pltpu.VMEM)
    hbm = pl.BlockSpec(memory_space=pltpu.HBM)
    rim = pltpu.VMEM((groups + 4, channels, LANES), BF16)
    edge = pltpu.VMEM((groups, channels, LANES), BF16)
    tile = pltpu.VMEM((channels, rows, LANES), BF16)
    line = (1, 3 * LANES)

    def kernel(*refs):
        body(rows, scale, *refs)

    act_c, grad_c, total = pl.pallas_call(
        kernel,
        out_shape=(
            jax.ShapeDtypeStruct(image.shape, BF16),
            jax.ShapeDtypeStruct(image.shape, BF16),
            jax.ShapeDtypeStruct((PLANE,) + line, F32),
        ),
        in_specs=[hbm] * 4,
        out_specs=(vmem, vmem, vmem),
        scratch_shapes=[
            pltpu.VMEM(weight.shape, BF16),
            pltpu.VMEM((1, channels), F32),
            pltpu.VMEM((channels, ext, LANES), BF16),
            tile,
            pltpu.VMEM((channels, rows * LANES), BF16),
            pltpu.VMEM((3 * channels, ext * LANES), BF16),
            pltpu.VMEM((3 * channels, ext * LANES), BF16),
            rim, rim, rim, rim, edge, edge,
            pltpu.VMEM((channels, rows * LANES), BF16),
            pltpu.VMEM((3, channels, LANES), F32),
            pltpu.VMEM((PLANE,) + line, F32),
            pltpu.VMEM((PLANE,) + line, F32),
            pltpu.VMEM((DEPTH,) + line, F32),
            pltpu.VMEM((2,) + line, F32),
            pltpu.SemaphoreType.DMA((4,)),
            pltpu.SemaphoreType.DMA((10,)),
            pltpu.SemaphoreType.DMA((10,)),
            pltpu.SemaphoreType.DMA((10,)),
            pltpu.SemaphoreType.DMA((10,)),
            pltpu.SemaphoreType.DMA((3,)),
            pltpu.SemaphoreType.DMA((3,)),
            pltpu.SemaphoreType.REGULAR,
            pltpu.SemaphoreType.REGULAR,
        ],
        compiler_params=pltpu.CompilerParams(
            collective_id=0, has_side_effects=True, vmem_limit_bytes=20 * 2**20
        ),
    )(*(pltpu.with_memory_space_constraint(v, pltpu.HBM) for v in (image, weight, bias.reshape(1, channels), cotangent)))
    act, grad, gw, gb = pl.pallas_call(
        write_out,
        out_shape=(
            jax.ShapeDtypeStruct(image.shape, BF16),
            jax.ShapeDtypeStruct(image.shape, BF16),
            jax.ShapeDtypeStruct(weight.shape, F32),
            jax.ShapeDtypeStruct((1, channels), F32),
        ),
        in_specs=[vmem] * 3,
        out_specs=(hbm, hbm, vmem, vmem),
        scratch_shapes=[pltpu.SemaphoreType.DMA((2,))],
        compiler_params=pltpu.CompilerParams(vmem_limit_bytes=8 * 2**20),
    )(act_c, grad_c, total)
    return act, grad, gw, gb.reshape(channels)


def solution(mesh):
    return jax.shard_map(
        shards,
        mesh=mesh,
        in_specs=(P(None, "row", "col"), P(), P(), P(None, "row", "col")),
        out_specs=(P(None, "row", "col"), P(None, "row", "col"), P(), P()),
        check_vma=False,
    )
```

```python
import math

import jax
import jax.numpy as jnp
from jax import lax
from jax.experimental import pallas as pl
from jax.experimental.pallas import tpu as pltpu
from jax.sharding import PartitionSpec as P

MESH = pl.DeviceIdType.MESH
BF16 = jnp.bfloat16
F32 = jnp.float32
DIL = 16
LANES = 128
PLANE = 32
DEPTH = 16
COEF = 0.7978845608
CUBIC = 0.044715


def ring_order(count):
    return sorted(range(1, count), key=lambda k: -min(k, count - k))


def gelu_pair(z):
    square = z * z
    t = jnp.tanh(z * (COEF + (COEF * CUBIC) * square))
    half = 0.5 + 0.5 * t
    bend = (1.0 - t * t) * (0.5 * COEF + (1.5 * COEF * CUBIC) * square)
    return z * half, half + z * bend


def lanes_of(row, count=1):
    return slice(row * LANES, (row + count) * LANES)


def body(
    rows, scale,
    image, weight_in, bias_in, cotangent,
    act_c, grad_c, total,
    weight, bias, xin, cin, cot, stack, gstack, xleft, xright, gleft, gright,
    cot_l, cot_r, act_l, act_r, grad_l, grad_r, act, accs,
    terms, gathered, layers, piece,
    local_sem, xsend, xrecv, gsend, grecv, rsend, rrecv, chain_a, chain_b,
):
    channels = image.shape[0]
    ext = rows + 2 * DIL
    groups = rows // 8
    row = lax.axis_index("row")
    col = lax.axis_index("col")
    nrow, ncol = lax.axis_size("row"), lax.axis_size("col")
    z = row % DEPTH
    y = (col // 8) * 2 + row // DEPTH
    x = (col // 2) % 4
    core = col % 2
    me = (row // DEPTH) * 16 + col

    def at(drow, dcol):
        return {"row": (row + drow + nrow) % nrow, "col": (col + dcol + ncol) % ncol}

    def deep(k):
        return {"row": (row // DEPTH) * DEPTH + (z + k + DEPTH) % DEPTH, "col": col}

    hops = lambda d: min(d, 4 - d)
    offsets = [(dy, dx, dc) for dy in range(4) for dx in range(4) for dc in range(2)][1:]
    offsets = sorted(offsets, key=lambda o: -(hops(o[0]) + hops(o[1])))
    plane = []
    for dy, dx, dc in offsets:
        py, px, pc = (y + dy) % 4, (x + dx) % 4, (core + dc) % 2
        pcol = (py // 2) * 8 + px * 2 + pc
        plane.append(({"row": (py % 2) * DEPTH + z, "col": pcol}, (py % 2) * 16 + pcol))

    barrier = pltpu.get_barrier_semaphore()
    greeted = [at(0, -1), at(0, 1), at(-1, 0), at(1, 0), at(-1, -1), at(-1, 1), at(1, -1), at(1, 1)]
    greeted += [deep(k) for k in (2, -2, 1, -1)]
    greeted += [peer for (peer, _), o in zip(plane, offsets) if hops(o[0]) + hops(o[1]) <= 2]
    for peer in greeted:
        pl.semaphore_signal(barrier, inc=1, device_id=peer, device_id_type=MESH)

    load_x = pltpu.make_async_copy(image, xin.at[:, DIL : DIL + rows, :], local_sem.at[0])
    load_c = pltpu.make_async_copy(cotangent, cin, local_sem.at[1])
    load_w = pltpu.make_async_copy(weight_in, weight, local_sem.at[2])
    load_b = pltpu.make_async_copy(bias_in, bias, local_sem.at[3])
    for load in (load_x, load_w, load_b, load_c):
        load.start()

    lane = lax.broadcasted_iota(jnp.int32, (channels, LANES), 1)
    slot = lane // DIL
    top, bottom = row == 0, row == nrow - 1
    first, last = col == 0, col == ncol - 1
    has = {
        "u": row > 0, "d": row < nrow - 1, "l": col > 0, "r": col < ncol - 1,
        "ul": (row > 0) & (col > 0), "ur": (row > 0) & (col < ncol - 1),
        "dl": (row < nrow - 1) & (col > 0), "dr": (row < nrow - 1) & (col < ncol - 1),
    }
    step = {
        "u0": (-1, 0), "d0": (1, 0), "u1": (-1, 0), "d1": (1, 0), "l": (0, -1), "r": (0, 1),
        "ul": (-1, -1), "ur": (-1, 1), "dl": (1, -1), "dr": (1, 1),
    }
    mirror = {
        "u0": "d0", "d0": "u0", "u1": "d1", "d1": "u1", "l": "r", "r": "l",
        "ul": "dr", "dr": "ul", "ur": "dl", "dl": "ur",
    }
    for n in ("u0", "u1", "d0", "d1"):
        has[n] = has[n[0]]
    names = list(step)
    vertical = ["d0", "u0", "d1", "u1"]
    sideways = ["l", "r", "ul", "ur", "dl", "dr"]

    low, center, high = (slice(k * channels, (k + 1) * channels) for k in range(3))
    above, below = lanes_of(0, 2), lanes_of(2 + groups, 2)
    level = lanes_of(2, groups)

    def halo_copies(top_src, bottom_src, top_dst, bottom_dst, own_l, own_r, left, right, send, recv):
        src_dst = {
            "u0": (top_src(0), bottom_dst(0)),
            "u1": (top_src(1), bottom_dst(1)),
            "d0": (bottom_src(0), top_dst(0)),
            "d1": (bottom_src(1), top_dst(1)),
            "l": (own_l(0, groups), right.at[:, level]),
            "r": (own_r(0, groups), left.at[:, level]),
            "ul": (own_l(0, 2), right.at[:, below]),
            "ur": (own_r(0, 2), left.at[:, below]),
            "dl": (own_l(groups - 2, 2), right.at[:, above]),
            "dr": (own_r(groups - 2, 2), left.at[:, above]),
        }
        return {
            n: pltpu.make_async_remote_copy(
                src, dst, send.at[names.index(n)], recv.at[names.index(n)],
                device_id=at(*step[n]), device_id_type=MESH,
            )
            for n, (src, dst) in src_dst.items()
        }

    def when_each(directions, predicate, action):
        for n in directions:
            pl.when(predicate(n))(lambda n=n: action(n))

    def send(copies, directions):
        when_each(directions, lambda n: has[n], lambda n: copies[n].start())

    def await_from(copies, directions):
        when_each(directions, lambda n: has[n], lambda n: copies[mirror[n]].wait_recv())

    def await_sent(copies):
        when_each(names, lambda n: has[n], lambda n: copies[n].wait_send())

    def clear(ref):
        ref[...] = jnp.zeros(ref.shape, ref.dtype)

    def zero_edges(left, right, top_dst, bottom_dst):
        pl.when(first)(lambda: clear(left))
        pl.when(last)(lambda: clear(right))

        @pl.when(top)
        def _():
            clear(top_dst)
            clear(left.at[:, above])
            clear(right.at[:, above])

        @pl.when(bottom)
        def _():
            clear(bottom_dst)
            clear(left.at[:, below])
            clear(right.at[:, below])

    def pack(source, part, r, column, target, to, g):
        merged = None
        for k in range(8):
            v = source[part, lanes_of(r + k)]
            turn = (DIL * k - column) % LANES
            v = pltpu.roll(v, turn, 1) if turn else v
            merged = v if merged is None else jnp.where(slot == k, v, merged)
        target[to, lanes_of(g)] = merged

    def unpack(target, part, r, left, right, g, k):
        a, b = left[:, lanes_of(g)], right[:, lanes_of(g)]
        a = pltpu.roll(a, LANES - DIL * k, 1) if k else a
        b = pltpu.roll(b, LANES - DIL - DIL * k, 1) if k < 7 else b
        v = target[part, lanes_of(r)]
        target[part, lanes_of(r)] = jnp.where(lane < DIL, a, jnp.where(lane >= LANES - DIL, b, v))

    def shift_row(source, r):
        v = source[center, lanes_of(r)]
        source[low, lanes_of(r)] = pltpu.roll(v, DIL, 1)
        source[high, lanes_of(r)] = pltpu.roll(v, LANES - DIL, 1)

    def merge_group(source, left, right, g):
        lv, rv = left[:, lanes_of(g)], right[:, lanes_of(g)]
        for k in range(8):
            r = lanes_of(8 * g + k)
            a = lv if k == 0 else pltpu.roll(lv, LANES - DIL * k, 1)
            b = rv if k == 7 else pltpu.roll(rv, LANES - DIL - DIL * k, 1)
            source[low, r] = jnp.where(lane < DIL, a, source[low, r])
            source[high, r] = jnp.where(lane >= LANES - DIL, b, source[high, r])

    def transpose_in(src, src_row, dst, part, dst_row, count=DIL):
        v = jnp.transpose(src[:, src_row : src_row + count, :], (1, 0, 2))
        for h in range(count):
            dst[part, lanes_of(dst_row + h)] = v[h]

    def transpose_out(value, dst, dst_row):
        v = jnp.stack([value[:, lanes_of(h)] for h in range(DIL)], axis=0)
        dst[:, dst_row : dst_row + DIL, :] = jnp.transpose(v, (1, 0, 2))

    bias_sum = [jnp.zeros((channels, LANES), F32)]

    def pixels(source, offsets, count, factor):
        z_val = offset
        for a in range(3):
            z_val = z_val + jnp.dot(
                forward[a], source[:, lanes_of(offsets[a], count)], preferred_element_type=F32
            )
        value, slope = gelu_pair(z_val)
        g = (factor.astype(F32) * slope).astype(BF16)
        wide = g.astype(F32)
        part = bias_sum[0]
        for h in range(count):
            part = part + wide[:, lanes_of(h)]
        bias_sum[0] = part
        return value.astype(BF16), g

    def forward_rows(r0, count):
        for r in range(r0, r0 + count, 4):
            value, g = pixels(stack, [r + DIL * a for a in range(3)], 4, cot[:, lanes_of(r, 4)])
            act[:, lanes_of(r, 4)] = value
            gstack[center, lanes_of(r + DIL, 4)] = g

    sides = ((xleft, cot_l, act_l, grad_l), (xright, cot_r, act_r, grad_r))

    def forward_edges(g0, count):
        for source, factor, value_to, grad_to in sides:
            for g in range(g0, g0 + count, 2):
                value, grad = pixels(source, [g + 2 * a for a in range(3)], 2, factor[:, lanes_of(g, 2)])
                value_to[:, lanes_of(g, 2)] = value
                grad_to[:, lanes_of(g, 2)] = grad

    def pixel_sum(left, right):
        return lax.dot_general(left, right, (((1,), (1,)), ((), ())), preferred_element_type=F32)

    def weight_rows(h0, count):
        for a in range(3):
            inner[a] = inner[a] + pixel_sum(
                gstack[center, lanes_of(DIL + h0, count)], stack[:, lanes_of(h0 + DIL * a, count)]
            )

    def weight_edges(g0, count):
        for source, _, _, grad in sides:
            for a in range(3):
                inner[a] = inner[a] + pixel_sum(
                    grad[:, lanes_of(g0, count)], source[:, lanes_of(g0 + 2 * a, count)]
                )

    def rows_of(ref, r0):
        return lambda k: ref.at[:, r0 + 8 * k : r0 + 8 * k + 8, :]

    def lines_of(r0):
        return lambda k: gstack.at[center, lanes_of(r0 + 8 * k, 8)]

    load_x.wait()
    for h in range(0, rows, DIL):
        transpose_in(xin, DIL + h, stack, center, DIL + h)
    for g in range(groups):
        pack(stack, center, DIL + 8 * g, 0, xleft, center, 2 + g)
        pack(stack, center, DIL + 8 * g, LANES - DIL, xright, center, 2 + g)

    pl.semaphore_wait(barrier, len(greeted))
    xcopies = halo_copies(
        rows_of(image, 0), rows_of(image, rows - DIL), rows_of(xin, 0), rows_of(xin, rows + DIL),
        lambda g, n: xleft.at[center, lanes_of(2 + g, n)],
        lambda g, n: xright.at[center, lanes_of(2 + g, n)],
        xleft.at[low], xright.at[high], xsend, xrecv,
    )
    send(xcopies, sideways[:2] + vertical + sideways[2:])
    chain = [peer for (peer, _), o in zip(plane, offsets) if o[0] % 2 and o[1] % 2 and o[2] == 0]
    chain += [deep(2), deep(-2)]
    for peer in chain:
        pl.semaphore_signal(chain_a, inc=1, device_id=peer, device_id_type=MESH)

    zero_edges(
        xleft.at[low], xright.at[high], xin.at[:, 0:DIL, :], xin.at[:, rows + DIL : ext, :]
    )
    for h in range(rows):
        shift_row(stack, DIL + h)
    load_c.wait()
    for h in range(0, rows, DIL):
        transpose_in(cin, h, cot, slice(0, channels), h)
    for g in range(groups):
        pack(cot, slice(0, channels), 8 * g, 0, cot_l, slice(0, channels), g)
        pack(cot, slice(0, channels), 8 * g, LANES - DIL, cot_r, slice(0, channels), g)
    inside = (lane >= DIL) & (lane < LANES - DIL)
    for h in range(rows):
        v = cot[:, lanes_of(h)]
        cot[:, lanes_of(h)] = jnp.where(inside, v, jnp.zeros_like(v))
    load_w.wait()
    load_b.wait()
    forward = [
        jnp.concatenate([weight[a, e] for e in range(3)], axis=1) for a in range(3)
    ]
    backward = [
        jnp.concatenate([weight[2 - a, 2 - e].T for e in range(3)], axis=1) for a in range(3)
    ]
    sub = lax.broadcasted_iota(jnp.int32, (channels, channels), 0)
    lan = lax.broadcasted_iota(jnp.int32, (channels, channels), 1)
    offset = jnp.sum(jnp.where(sub == lan, bias[...], 0.0), axis=1, keepdims=True)
    accs[...] = jnp.zeros_like(accs)


    forward_rows(DIL, rows - 2 * DIL)
    blocks = [gstack[center, lanes_of(DIL + h, DIL)] for h in range(DIL, rows - DIL, DIL)]
    none = jnp.zeros_like(blocks[0])
    stacked = None
    for k in range(len(blocks) + 2):
        lines = [blocks[k - a] if 0 <= k - a < len(blocks) else none for a in range(3)]
        d = lax.dot_general(
            jnp.concatenate(lines, axis=0),
            stack[:, lanes_of((k + 1) * DIL, DIL)],
            (((1,), (1,)), ((), ())),
            preferred_element_type=F32,
        )
        stacked = d if stacked is None else stacked + d
    inner = [stacked[a * channels : (a + 1) * channels] for a in range(3)]

    for g in range(groups):
        pack(stack, center, DIL + 8 * g, DIL, xleft, high, 2 + g)
        pack(stack, center, DIL + 8 * g, LANES - 2 * DIL, xright, low, 2 + g)

    def rim(k):
        await_from(xcopies, [f"u{k}", f"d{k}"])
        for base, g in ((8 * k, k), (rows + DIL + 8 * k, 2 + groups + k)):
            transpose_in(xin, base, stack, center, base, 8)
            for h in range(8):
                shift_row(stack, base + h)
        for r in (8 * k, rows - DIL + 8 * k):
            forward_rows(r, 8)
            weight_rows(r, 8)
        for base, g in ((8 * k, k), (rows + DIL + 8 * k, 2 + groups + k)):
            pack(stack, center, base, 0, xleft, center, g)
            pack(stack, center, base, DIL, xleft, high, g)
            pack(stack, center, base, LANES - 2 * DIL, xright, low, g)
            pack(stack, center, base, LANES - DIL, xright, center, g)

    rim(0)
    await_from(xcopies, ["l", "r"])
    forward_edges(2, groups - 4)
    weight_edges(2, groups - 4)
    rim(1)
    await_from(xcopies, ["ul", "ur", "dl", "dr"])
    for g in (0, groups - 2):
        forward_edges(g, 2)
        weight_edges(g, 2)
    for a in range(3):
        accs[a, :, 0 : 3 * channels] = inner[a]
    accs[0, :, 3 * channels : 3 * channels + 1] = jnp.sum(bias_sum[0], axis=1, keepdims=True)
    for a in range(3):
        terms[:, 0, lanes_of(a)] = accs[a]
    pl.semaphore_wait(chain_a, len(chain))
    for k in (4, -4):
        pl.semaphore_signal(chain_b, inc=1, device_id=deep(k), device_id_type=MESH)

    def remote(src, dst, k, peer):
        pltpu.make_async_remote_copy(
            src, dst, rsend.at[k], rrecv.at[k], device_id=peer, device_id_type=MESH
        ).start()

    def drain(sem, buffer):
        pltpu.make_async_copy(buffer, buffer, sem).wait()

    for peer, index in plane:
        remote(terms.at[index], gathered.at[me], 0, peer)
    gathered[me] = terms[me]

    gcopies = halo_copies(
        lines_of(DIL), lines_of(rows), lines_of(0), lines_of(rows + DIL),
        lambda g, n: grad_l.at[:, lanes_of(g, n)],
        lambda g, n: grad_r.at[:, lanes_of(g, n)],
        gleft, gright, gsend, grecv,
    )
    send(gcopies, sideways)
    rim_first = [r for r in range(rows) if r < DIL or r >= rows - DIL]
    rim_first += [r for r in range(DIL, rows - DIL)]
    for n, r in enumerate(rim_first):
        unpack(gstack, center, DIL + r, grad_l, grad_r, r // 8, r % 8)
        if n == 2 * DIL - 1:
            send(gcopies, vertical)
    for r in range(rows):
        unpack(act, slice(0, channels), r, act_l, act_r, r // 8, r % 8)
    zero_edges(
        gleft, gright,
        gstack.at[center, lanes_of(0, DIL)], gstack.at[center, lanes_of(rows + DIL, DIL)],
    )
    for h in range(0, rows, DIL):
        transpose_out(act[:, lanes_of(h, DIL)], act_c, h)
    for h in range(rows):
        shift_row(gstack, DIL + h)
    pl.semaphore_wait(chain_b, 2)

    drain(rrecv.at[0], gathered.at[pl.ds(0, PLANE - 1)])
    piece[0] = jnp.sum(gathered[...], axis=0)
    for k in ring_order(DEPTH):
        remote(piece.at[0], layers.at[z], 1, deep(k))
    layers[z] = piece[0]

    await_from(gcopies, names)
    for base in (0, rows + DIL):
        for h in range(DIL):
            shift_row(gstack, base + h)
    for g in range(4 + groups):
        merge_group(gstack, gleft, gright, g)
    for h in range(0, rows, DIL):
        tiles = []
        for r in (h, h + 8):
            out = None
            for a in range(3):
                d = jnp.dot(
                    backward[a], gstack[:, lanes_of(r + DIL * a, 8)], preferred_element_type=F32
                )
                out = d if out is None else out + d
            tiles.append(out.astype(BF16))
        transpose_out(jnp.concatenate(tiles, axis=1), grad_c, h)

    drain(rrecv.at[1], layers.at[pl.ds(0, DEPTH - 1)])
    piece[1] = jnp.sum(layers[...], axis=0) * scale
    for peer, index in plane:
        remote(piece.at[1], total.at[me], 2, peer)
    total[me] = piece[1]
    await_sent(xcopies)
    await_sent(gcopies)
    drain(rsend.at[0], gathered.at[pl.ds(0, PLANE - 1)])
    drain(rsend.at[1], layers.at[pl.ds(0, DEPTH - 1)])
    drain(rrecv.at[2], total.at[pl.ds(0, PLANE - 1)])
    drain(rsend.at[2], total.at[pl.ds(0, PLANE - 1)])


def write_out(act_c, grad_c, total, act_out, grad_out, gw_out, gb_out, gw, gb, sem):
    channels = act_c.shape[0]
    copies = [
        pltpu.make_async_copy(act_c, act_out, sem.at[0]),
        pltpu.make_async_copy(grad_c, grad_out, sem.at[1]),
        pltpu.make_async_copy(gw, gw_out, sem.at[2]),
        pltpu.make_async_copy(gb, gb_out, sem.at[3]),
    ]
    copies[0].start()
    copies[1].start()
    sub = lax.broadcasted_iota(jnp.int32, (channels, channels), 0)
    lan = lax.broadcasted_iota(jnp.int32, (channels, channels), 1)
    for a in range(3):
        tile = total[:, 0, lanes_of(a)]
        for e in range(3):
            gw[a, e] = tile[:, e * channels : (e + 1) * channels]
        if a == 0:
            column = tile[:, 3 * channels : 3 * channels + 1]
            gb[...] = jnp.sum(jnp.where(sub == lan, column, 0.0), axis=0, keepdims=True)
    copies[2].start()
    copies[3].start()
    for copy in copies:
        copy.wait()


def shards(image, weight, bias, cotangent):
    channels, rows, columns = image.shape
    assert columns == LANES and rows % DIL == 0 and channels == PLANE
    count = rows * lax.axis_size("row") * columns * lax.axis_size("col")
    scale = 1.0 / math.sqrt(count)
    ext = rows + 2 * DIL
    groups = rows // 8
    vmem = pl.BlockSpec(memory_space=pltpu.VMEM)
    hbm = pl.BlockSpec(memory_space=pltpu.HBM)
    taps = pltpu.VMEM((3 * channels, (groups + 4) * LANES), BF16)
    rim = pltpu.VMEM((channels, (groups + 4) * LANES), BF16)
    edge = pltpu.VMEM((channels, groups * LANES), BF16)
    tile = pltpu.VMEM((channels, rows, LANES), BF16)
    line = (1, 3 * LANES)

    def kernel(*refs):
        body(rows, scale, *refs)

    act_c, grad_c, total = pl.pallas_call(
        kernel,
        out_shape=(
            jax.ShapeDtypeStruct(image.shape, BF16),
            jax.ShapeDtypeStruct(image.shape, BF16),
            jax.ShapeDtypeStruct((PLANE,) + line, F32),
        ),
        in_specs=[hbm] * 4,
        out_specs=(vmem, vmem, vmem),
        scratch_shapes=[
            pltpu.VMEM(weight.shape, BF16),
            pltpu.VMEM((1, channels), F32),
            pltpu.VMEM((channels, ext, LANES), BF16),
            tile,
            pltpu.VMEM((channels, rows * LANES), BF16),
            pltpu.VMEM((3 * channels, ext * LANES), BF16),
            pltpu.VMEM((3 * channels, ext * LANES), BF16),
            taps, taps, rim, rim, edge, edge, edge, edge, edge, edge,
            pltpu.VMEM((channels, rows * LANES), BF16),
            pltpu.VMEM((3, channels, LANES), F32),
            pltpu.VMEM((PLANE,) + line, F32),
            pltpu.VMEM((PLANE,) + line, F32),
            pltpu.VMEM((DEPTH,) + line, F32),
            pltpu.VMEM((2,) + line, F32),
            pltpu.SemaphoreType.DMA((4,)),
            pltpu.SemaphoreType.DMA((10,)),
            pltpu.SemaphoreType.DMA((10,)),
            pltpu.SemaphoreType.DMA((10,)),
            pltpu.SemaphoreType.DMA((10,)),
            pltpu.SemaphoreType.DMA((3,)),
            pltpu.SemaphoreType.DMA((3,)),
            pltpu.SemaphoreType.REGULAR,
            pltpu.SemaphoreType.REGULAR,
        ],
        compiler_params=pltpu.CompilerParams(
            collective_id=0, has_side_effects=True, vmem_limit_bytes=20 * 2**20
        ),
    )(*(pltpu.with_memory_space_constraint(v, pltpu.HBM) for v in (image, weight, bias.reshape(1, channels), cotangent)))
    act, grad, gw, gb = pl.pallas_call(
        write_out,
        out_shape=(
            jax.ShapeDtypeStruct(image.shape, BF16),
            jax.ShapeDtypeStruct(image.shape, BF16),
            jax.ShapeDtypeStruct(weight.shape, F32),
            jax.ShapeDtypeStruct((1, channels), F32),
        ),
        in_specs=[vmem] * 3,
        out_specs=(hbm, hbm, hbm, hbm),
        scratch_shapes=[
            pltpu.VMEM(weight.shape, F32),
            pltpu.VMEM((1, channels), F32),
            pltpu.SemaphoreType.DMA((4,)),
        ],
        compiler_params=pltpu.CompilerParams(vmem_limit_bytes=8 * 2**20),
    )(act_c, grad_c, total)
    return act, grad, gw, gb.reshape(channels)


def solution(mesh):
    return jax.shard_map(
        shards,
        mesh=mesh,
        in_specs=(P(None, "row", "col"), P(), P(), P(None, "row", "col")),
        out_specs=(P(None, "row", "col"), P(None, "row", "col"), P(), P()),
        check_vma=False,
    )
```

```python
import math

import jax
import jax.numpy as jnp
from jax import lax
from jax.experimental import pallas as pl
from jax.experimental.pallas import tpu as pltpu
from jax.sharding import PartitionSpec as P

MESH = pl.DeviceIdType.MESH
BF16 = jnp.bfloat16
F32 = jnp.float32
DIL = 16
LANES = 128
PLANE = 32
DEPTH = 16
COEF = 0.7978845608
CUBIC = 0.044715


def ring_order(count):
    return sorted(range(1, count), key=lambda k: -min(k, count - k))


def gelu_pair(z):
    square = z * z
    t = jnp.tanh(z * (COEF + (COEF * CUBIC) * square))
    half = 0.5 + 0.5 * t
    bend = (1.0 - t * t) * (0.5 * COEF + (1.5 * COEF * CUBIC) * square)
    return z * half, half + z * bend


def lanes_of(row, count=1):
    return slice(row * LANES, (row + count) * LANES)


def body(
    rows, scale,
    image, weight_in, bias_in, cotangent,
    act_c, grad_c, total,
    weight, bias, xin, cin, cot, stack, gstack, xside, gleft, gright,
    cot_s, act_s, grad_s, act, accs,
    terms, gathered, layers, piece,
    local_sem, xsend, xrecv, gsend, grecv, rsend, rrecv, chain_a, chain_b, chain_c,
):
    xleft, xright = xside.at[0], xside.at[1]
    cot_l, cot_r = cot_s.at[0], cot_s.at[1]
    act_l, act_r = act_s.at[0], act_s.at[1]
    grad_l, grad_r = grad_s.at[0], grad_s.at[1]
    channels = image.shape[0]
    ext = rows + 2 * DIL
    groups = rows // 8
    row = lax.axis_index("row")
    col = lax.axis_index("col")
    nrow, ncol = lax.axis_size("row"), lax.axis_size("col")
    z = row % DEPTH
    y = (col // 8) * 2 + row // DEPTH
    x = (col // 2) % 4
    core = col % 2
    me = (row // DEPTH) * 16 + col

    def at(drow, dcol):
        return {"row": (row + drow + nrow) % nrow, "col": (col + dcol + ncol) % ncol}

    def deep(k):
        return {"row": (row // DEPTH) * DEPTH + (z + k + DEPTH) % DEPTH, "col": col}

    hops = lambda d: min(d, 4 - d)
    offsets = [(dy, dx, dc) for dy in range(4) for dx in range(4) for dc in range(2)][1:]
    offsets = sorted(offsets, key=lambda o: -(hops(o[0]) + hops(o[1])))
    plane = []
    for dy, dx, dc in offsets:
        py, px, pc = (y + dy) % 4, (x + dx) % 4, (core + dc) % 2
        pcol = (py // 2) * 8 + px * 2 + pc
        plane.append(({"row": (py % 2) * DEPTH + z, "col": pcol}, (py % 2) * 16 + pcol))

    barrier = pltpu.get_barrier_semaphore()
    beside = [at(-1, 0), at(1, 0)]
    greeted = [at(0, -1), at(0, 1)] + beside
    greeted += [deep(k) for k in (2, -2, 1, -1)]
    greeted += [peer for (peer, _), o in zip(plane, offsets) if hops(o[0]) + hops(o[1]) <= 2]
    for peer in greeted:
        pl.semaphore_signal(barrier, inc=1, device_id=peer, device_id_type=MESH)

    load_x = pltpu.make_async_copy(image, xin.at[:, DIL : DIL + rows, :], local_sem.at[0])
    load_c = pltpu.make_async_copy(cotangent, cin, local_sem.at[1])
    load_w = pltpu.make_async_copy(weight_in, weight, local_sem.at[2])
    load_b = pltpu.make_async_copy(bias_in, bias, local_sem.at[3])
    for load in (load_x, load_w, load_b, load_c):
        load.start()

    lane = lax.broadcasted_iota(jnp.int32, (channels, LANES), 1)
    slot = lane // DIL
    top, bottom = row == 0, row == nrow - 1
    first, last = col == 0, col == ncol - 1
    has = {
        "u": row > 0, "d": row < nrow - 1, "l": col > 0, "r": col < ncol - 1,
        "ul": (row > 0) & (col > 0), "ur": (row > 0) & (col < ncol - 1),
        "dl": (row < nrow - 1) & (col > 0), "dr": (row < nrow - 1) & (col < ncol - 1),
    }
    step = {
        "u0": (-1, 0), "d0": (1, 0), "u1": (-1, 0), "d1": (1, 0), "l": (0, -1), "r": (0, 1),
        "ul": (-1, -1), "ur": (-1, 1), "dl": (1, -1), "dr": (1, 1),
    }
    mirror = {
        "u0": "d0", "d0": "u0", "u1": "d1", "d1": "u1", "l": "r", "r": "l",
        "ul": "dr", "dr": "ul", "ur": "dl", "dl": "ur",
    }
    for n in ("u0", "u1", "d0", "d1"):
        has[n] = has[n[0]]
    names = list(step)
    vertical = ["d0", "u0", "d1", "u1"]
    sideways = ["l", "r", "ul", "ur", "dl", "dr"]

    low, center, high = (slice(k * channels, (k + 1) * channels) for k in range(3))
    above, below = lanes_of(0, 2), lanes_of(2 + groups, 2)
    level = lanes_of(2, groups)

    def halo_copies(top_src, bottom_src, top_dst, bottom_dst, own_l, own_r, left, right, send, recv):
        src_dst = {
            "u0": (top_src(0), bottom_dst(0)),
            "u1": (top_src(1), bottom_dst(1)),
            "d0": (bottom_src(0), top_dst(0)),
            "d1": (bottom_src(1), top_dst(1)),
            "l": (own_l(0, groups), right.at[:, level]),
            "r": (own_r(0, groups), left.at[:, level]),
            "ul": (own_l(0, 2), right.at[:, below]),
            "ur": (own_r(0, 2), left.at[:, below]),
            "dl": (own_l(groups - 2, 2), right.at[:, above]),
            "dr": (own_r(groups - 2, 2), left.at[:, above]),
        }
        return {
            n: pltpu.make_async_remote_copy(
                src, dst, send.at[names.index(n)], recv.at[names.index(n)],
                device_id=at(*step[n]), device_id_type=MESH,
            )
            for n, (src, dst) in src_dst.items()
        }

    def when_each(directions, predicate, action):
        for n in directions:
            pl.when(predicate(n))(lambda n=n: action(n))

    def send(copies, directions):
        when_each(directions, lambda n: has[n], lambda n: copies[n].start())

    def await_from(copies, directions):
        when_each(directions, lambda n: has[n], lambda n: copies[mirror[n]].wait_recv())

    def await_sent(copies):
        when_each(names, lambda n: has[n], lambda n: copies[n].wait_send())

    def clear(ref):
        ref[...] = jnp.zeros(ref.shape, ref.dtype)

    def zero_edges(left, right, top_dst, bottom_dst):
        pl.when(first)(lambda: clear(left))
        pl.when(last)(lambda: clear(right))

        @pl.when(top)
        def _():
            clear(top_dst)
            clear(left.at[:, above])
            clear(right.at[:, above])

        @pl.when(bottom)
        def _():
            clear(bottom_dst)
            clear(left.at[:, below])
            clear(right.at[:, below])

    def pack(source, part, r, column, target, to, g):
        merged = None
        for k in range(8):
            v = source[part, lanes_of(r + k)]
            turn = (DIL * k - column) % LANES
            v = pltpu.roll(v, turn, 1) if turn else v
            merged = v if merged is None else jnp.where(slot == k, v, merged)
        target[to, lanes_of(g)] = merged

    def unpack(target, part, r, left, right, g, k):
        a, b = left[:, lanes_of(g)], right[:, lanes_of(g)]
        a = pltpu.roll(a, LANES - DIL * k, 1) if k else a
        b = pltpu.roll(b, LANES - DIL - DIL * k, 1) if k < 7 else b
        v = target[part, lanes_of(r)]
        target[part, lanes_of(r)] = jnp.where(lane < DIL, a, jnp.where(lane >= LANES - DIL, b, v))

    def shift_row(source, r):
        v = source[center, lanes_of(r)]
        source[low, lanes_of(r)] = pltpu.roll(v, DIL, 1)
        source[high, lanes_of(r)] = pltpu.roll(v, LANES - DIL, 1)

    def merge_group(source, left, right, g):
        lv, rv = left[:, lanes_of(g)], right[:, lanes_of(g)]
        for k in range(8):
            r = lanes_of(8 * g + k)
            a = lv if k == 0 else pltpu.roll(lv, LANES - DIL * k, 1)
            b = rv if k == 7 else pltpu.roll(rv, LANES - DIL - DIL * k, 1)
            source[low, r] = jnp.where(lane < DIL, a, source[low, r])
            source[high, r] = jnp.where(lane >= LANES - DIL, b, source[high, r])

    def transpose_in(src, src_row, dst, part, dst_row, count=DIL):
        v = jnp.transpose(src[:, src_row : src_row + count, :], (1, 0, 2))
        for h in range(count):
            dst[part, lanes_of(dst_row + h)] = v[h]

    def transpose_out(value, dst, dst_row):
        v = jnp.stack([value[:, lanes_of(h)] for h in range(DIL)], axis=0)
        dst[:, dst_row : dst_row + DIL, :] = jnp.transpose(v, (1, 0, 2))

    bias_sum = [jnp.zeros((channels, LANES), F32)]

    def pixels(source, offsets, count, factor):
        z_val = offset
        for a in range(3):
            z_val = z_val + jnp.dot(
                forward[a], source[:, lanes_of(offsets[a], count)], preferred_element_type=F32
            )
        value, slope = gelu_pair(z_val)
        g = (factor.astype(F32) * slope).astype(BF16)
        wide = g.astype(F32)
        part = bias_sum[0]
        for h in range(count):
            part = part + wide[:, lanes_of(h)]
        bias_sum[0] = part
        return value.astype(BF16), g

    def forward_rows(r0, count):
        for r in range(r0, r0 + count, 4):
            value, g = pixels(stack, [r + DIL * a for a in range(3)], 4, cot[:, lanes_of(r, 4)])
            act[:, lanes_of(r, 4)] = value
            gstack[center, lanes_of(r + DIL, 4)] = g

    early, late = 1 - core, core

    def forward_edges(side, g0, count):
        source, factor = xside.at[side], cot_s.at[side]
        for g in range(g0, g0 + count, 2):
            value, grad = pixels(source, [g + 2 * a for a in range(3)], 2, factor[:, lanes_of(g, 2)])
            act_s[side, :, lanes_of(g, 2)] = value
            grad_s[side, :, lanes_of(g, 2)] = grad

    def pixel_sum(left, right):
        return lax.dot_general(left, right, (((1,), (1,)), ((), ())), preferred_element_type=F32)

    def weight_rows(h0, count):
        for a in range(3):
            inner[a] = inner[a] + pixel_sum(
                gstack[center, lanes_of(DIL + h0, count)], stack[:, lanes_of(h0 + DIL * a, count)]
            )

    def weight_edges(side, g0, count):
        for a in range(3):
            inner[a] = inner[a] + pixel_sum(
                grad_s[side, :, lanes_of(g0, count)], xside[side, :, lanes_of(g0 + 2 * a, count)]
            )

    def rows_of(ref, r0):
        return lambda k: ref.at[:, r0 + 8 * k : r0 + 8 * k + 8, :]

    def lines_of(r0):
        return lambda k: gstack.at[center, lanes_of(r0 + 8 * k, 8)]

    load_x.wait()
    for h in range(0, rows, DIL):
        transpose_in(xin, DIL + h, stack, center, DIL + h)
    for g in range(groups):
        pack(stack, center, DIL + 8 * g, 0, xleft, center, 2 + g)
        pack(stack, center, DIL + 8 * g, LANES - DIL, xright, center, 2 + g)

    pl.semaphore_wait(barrier, len(greeted))
    xcopies = halo_copies(
        rows_of(image, 0), rows_of(image, rows - DIL), rows_of(xin, 0), rows_of(xin, rows + DIL),
        lambda g, n: xleft.at[center, lanes_of(2 + g, n)],
        lambda g, n: xright.at[center, lanes_of(2 + g, n)],
        xleft.at[low], xright.at[high], xsend, xrecv,
    )
    for peer in beside:
        pl.semaphore_signal(chain_c, inc=1, device_id=peer, device_id_type=MESH)
    send(xcopies, sideways[:2] + vertical)
    chain = [peer for (peer, _), o in zip(plane, offsets) if o[0] % 2 and o[1] % 2 and o[2] == 0]
    chain += [deep(2), deep(-2)]
    for peer in chain:
        pl.semaphore_signal(chain_a, inc=1, device_id=peer, device_id_type=MESH)

    zero_edges(
        xleft.at[low], xright.at[high], xin.at[:, 0:DIL, :], xin.at[:, rows + DIL : ext, :]
    )
    for h in range(rows):
        shift_row(stack, DIL + h)
    pl.semaphore_wait(chain_c, len(beside))
    send(xcopies, sideways[2:])
    load_c.wait()
    for h in range(0, rows, DIL):
        transpose_in(cin, h, cot, slice(0, channels), h)
    for g in range(groups):
        pack(cot, slice(0, channels), 8 * g, 0, cot_l, slice(0, channels), g)
        pack(cot, slice(0, channels), 8 * g, LANES - DIL, cot_r, slice(0, channels), g)
    inside = (lane >= DIL) & (lane < LANES - DIL)
    for h in range(rows):
        v = cot[:, lanes_of(h)]
        cot[:, lanes_of(h)] = jnp.where(inside, v, jnp.zeros_like(v))
    load_w.wait()
    load_b.wait()
    forward = [
        jnp.concatenate([weight[a, e] for e in range(3)], axis=1) for a in range(3)
    ]
    backward = [
        jnp.concatenate([weight[2 - a, 2 - e].T for e in range(3)], axis=1) for a in range(3)
    ]
    sub = lax.broadcasted_iota(jnp.int32, (channels, channels), 0)
    lan = lax.broadcasted_iota(jnp.int32, (channels, channels), 1)
    offset = jnp.sum(jnp.where(sub == lan, bias[...], 0.0), axis=1, keepdims=True)
    accs[...] = jnp.zeros_like(accs)


    forward_rows(DIL, rows - 2 * DIL)
    blocks = [gstack[center, lanes_of(DIL + h, DIL)] for h in range(DIL, rows - DIL, DIL)]
    none = jnp.zeros_like(blocks[0])
    stacked = None
    for k in range(len(blocks) + 2):
        lines = [blocks[k - a] if 0 <= k - a < len(blocks) else none for a in range(3)]
        d = lax.dot_general(
            jnp.concatenate(lines, axis=0),
            stack[:, lanes_of((k + 1) * DIL, DIL)],
            (((1,), (1,)), ((), ())),
            preferred_element_type=F32,
        )
        stacked = d if stacked is None else stacked + d
    inner = [stacked[a * channels : (a + 1) * channels] for a in range(3)]

    for g in range(groups):
        pack(stack, center, DIL + 8 * g, DIL, xleft, high, 2 + g)
        pack(stack, center, DIL + 8 * g, LANES - 2 * DIL, xright, low, 2 + g)

    def rim(k):
        await_from(xcopies, [f"u{k}", f"d{k}"])
        for base, g in ((8 * k, k), (rows + DIL + 8 * k, 2 + groups + k)):
            transpose_in(xin, base, stack, center, base, 8)
            for h in range(8):
                shift_row(stack, base + h)
        for r in (8 * k, rows - DIL + 8 * k):
            forward_rows(r, 8)
            weight_rows(r, 8)
        for base, g in ((8 * k, k), (rows + DIL + 8 * k, 2 + groups + k)):
            pack(stack, center, base, 0, xleft, center, g)
            pack(stack, center, base, DIL, xleft, high, g)
            pack(stack, center, base, LANES - 2 * DIL, xright, low, g)
            pack(stack, center, base, LANES - DIL, xright, center, g)

    def await_side(right):
        pl.when(right & has["r"])(lambda: xcopies[mirror["r"]].wait_recv())
        pl.when(jnp.logical_not(right) & has["l"])(lambda: xcopies[mirror["l"]].wait_recv())

    rim(0)
    await_side(early == 1)
    forward_edges(early, 2, groups - 4)
    weight_edges(early, 2, groups - 4)
    rim(1)
    await_side(late == 1)
    forward_edges(late, 2, groups - 4)
    weight_edges(late, 2, groups - 4)
    await_from(xcopies, ["ul", "ur", "dl", "dr"])
    for side in (0, 1):
        for g in (0, groups - 2):
            forward_edges(side, g, 2)
            weight_edges(side, g, 2)
    for a in range(3):
        accs[a, :, 0 : 3 * channels] = inner[a]
    accs[0, :, 3 * channels : 3 * channels + 1] = jnp.sum(bias_sum[0], axis=1, keepdims=True)
    for a in range(3):
        terms[:, 0, lanes_of(a)] = accs[a]
    pl.semaphore_wait(chain_a, len(chain))
    for k in (4, -4):
        pl.semaphore_signal(chain_b, inc=1, device_id=deep(k), device_id_type=MESH)

    def remote(src, dst, k, peer):
        pltpu.make_async_remote_copy(
            src, dst, rsend.at[k], rrecv.at[k], device_id=peer, device_id_type=MESH
        ).start()

    def drain(sem, buffer):
        pltpu.make_async_copy(buffer, buffer, sem).wait()

    for peer, index in plane:
        remote(terms.at[index], gathered.at[me], 0, peer)
    gathered[me] = terms[me]

    gcopies = halo_copies(
        lines_of(DIL), lines_of(rows), lines_of(0), lines_of(rows + DIL),
        lambda g, n: grad_l.at[:, lanes_of(g, n)],
        lambda g, n: grad_r.at[:, lanes_of(g, n)],
        gleft, gright, gsend, grecv,
    )
    send(gcopies, sideways)
    rim_first = [r for r in range(rows) if r < DIL or r >= rows - DIL]
    rim_first += [r for r in range(DIL, rows - DIL)]
    for n, r in enumerate(rim_first):
        unpack(gstack, center, DIL + r, grad_l, grad_r, r // 8, r % 8)
        if n == 2 * DIL - 1:
            send(gcopies, vertical)
    for r in range(rows):
        unpack(act, slice(0, channels), r, act_l, act_r, r // 8, r % 8)
    zero_edges(
        gleft, gright,
        gstack.at[center, lanes_of(0, DIL)], gstack.at[center, lanes_of(rows + DIL, DIL)],
    )
    for h in range(0, rows, DIL):
        transpose_out(act[:, lanes_of(h, DIL)], act_c, h)
    for h in range(rows):
        shift_row(gstack, DIL + h)
    pl.semaphore_wait(chain_b, 2)

    drain(rrecv.at[0], gathered.at[pl.ds(0, PLANE - 1)])
    piece[0] = jnp.sum(gathered[...], axis=0)
    for k in ring_order(DEPTH):
        remote(piece.at[0], layers.at[z], 1, deep(k))
    layers[z] = piece[0]

    await_from(gcopies, names)
    for base in (0, rows + DIL):
        for h in range(DIL):
            shift_row(gstack, base + h)
    for g in range(4 + groups):
        merge_group(gstack, gleft, gright, g)
    for h in range(0, rows, DIL):
        tiles = []
        for r in (h, h + 8):
            out = None
            for a in range(3):
                d = jnp.dot(
                    backward[a], gstack[:, lanes_of(r + DIL * a, 8)], preferred_element_type=F32
                )
                out = d if out is None else out + d
            tiles.append(out.astype(BF16))
        transpose_out(jnp.concatenate(tiles, axis=1), grad_c, h)

    drain(rrecv.at[1], layers.at[pl.ds(0, DEPTH - 1)])
    piece[1] = jnp.sum(layers[...], axis=0) * scale
    for peer, index in plane:
        remote(piece.at[1], total.at[me], 2, peer)
    total[me] = piece[1]
    await_sent(xcopies)
    await_sent(gcopies)
    drain(rsend.at[0], gathered.at[pl.ds(0, PLANE - 1)])
    drain(rsend.at[1], layers.at[pl.ds(0, DEPTH - 1)])
    drain(rrecv.at[2], total.at[pl.ds(0, PLANE - 1)])
    drain(rsend.at[2], total.at[pl.ds(0, PLANE - 1)])


def write_out(act_c, grad_c, total, act_out, grad_out, gw_out, gb_out, gw, gb, sem):
    channels = act_c.shape[0]
    copies = [
        pltpu.make_async_copy(act_c, act_out, sem.at[0]),
        pltpu.make_async_copy(grad_c, grad_out, sem.at[1]),
        pltpu.make_async_copy(gw, gw_out, sem.at[2]),
        pltpu.make_async_copy(gb, gb_out, sem.at[3]),
    ]
    copies[0].start()
    copies[1].start()
    sub = lax.broadcasted_iota(jnp.int32, (channels, channels), 0)
    lan = lax.broadcasted_iota(jnp.int32, (channels, channels), 1)
    for a in range(3):
        tile = total[:, 0, lanes_of(a)]
        for e in range(3):
            gw[a, e] = tile[:, e * channels : (e + 1) * channels]
        if a == 0:
            column = tile[:, 3 * channels : 3 * channels + 1]
            gb[...] = jnp.sum(jnp.where(sub == lan, column, 0.0), axis=0, keepdims=True)
    copies[2].start()
    copies[3].start()
    for copy in copies:
        copy.wait()


def shards(image, weight, bias, cotangent):
    channels, rows, columns = image.shape
    assert columns == LANES and rows % DIL == 0 and channels == PLANE
    count = rows * lax.axis_size("row") * columns * lax.axis_size("col")
    scale = 1.0 / math.sqrt(count)
    ext = rows + 2 * DIL
    groups = rows // 8
    vmem = pl.BlockSpec(memory_space=pltpu.VMEM)
    hbm = pl.BlockSpec(memory_space=pltpu.HBM)
    taps = pltpu.VMEM((2, 3 * channels, (groups + 4) * LANES), BF16)
    rim = pltpu.VMEM((channels, (groups + 4) * LANES), BF16)
    edge = pltpu.VMEM((2, channels, groups * LANES), BF16)
    tile = pltpu.VMEM((channels, rows, LANES), BF16)
    line = (1, 3 * LANES)

    def kernel(*refs):
        body(rows, scale, *refs)

    act_c, grad_c, total = pl.pallas_call(
        kernel,
        out_shape=(
            jax.ShapeDtypeStruct(image.shape, BF16),
            jax.ShapeDtypeStruct(image.shape, BF16),
            jax.ShapeDtypeStruct((PLANE,) + line, F32),
        ),
        in_specs=[hbm] * 4,
        out_specs=(vmem, vmem, vmem),
        scratch_shapes=[
            pltpu.VMEM(weight.shape, BF16),
            pltpu.VMEM((1, channels), F32),
            pltpu.VMEM((channels, ext, LANES), BF16),
            tile,
            pltpu.VMEM((channels, rows * LANES), BF16),
            pltpu.VMEM((3 * channels, ext * LANES), BF16),
            pltpu.VMEM((3 * channels, ext * LANES), BF16),
            taps, rim, rim, edge, edge, edge,
            pltpu.VMEM((channels, rows * LANES), BF16),
            pltpu.VMEM((3, channels, LANES), F32),
            pltpu.VMEM((PLANE,) + line, F32),
            pltpu.VMEM((PLANE,) + line, F32),
            pltpu.VMEM((DEPTH,) + line, F32),
            pltpu.VMEM((2,) + line, F32),
            pltpu.SemaphoreType.DMA((4,)),
            pltpu.SemaphoreType.DMA((10,)),
            pltpu.SemaphoreType.DMA((10,)),
            pltpu.SemaphoreType.DMA((10,)),
            pltpu.SemaphoreType.DMA((10,)),
            pltpu.SemaphoreType.DMA((3,)),
            pltpu.SemaphoreType.DMA((3,)),
            pltpu.SemaphoreType.REGULAR,
            pltpu.SemaphoreType.REGULAR,
            pltpu.SemaphoreType.REGULAR,
        ],
        compiler_params=pltpu.CompilerParams(
            collective_id=0, has_side_effects=True, vmem_limit_bytes=20 * 2**20
        ),
    )(*(pltpu.with_memory_space_constraint(v, pltpu.HBM) for v in (image, weight, bias.reshape(1, channels), cotangent)))
    act, grad, gw, gb = pl.pallas_call(
        write_out,
        out_shape=(
            jax.ShapeDtypeStruct(image.shape, BF16),
            jax.ShapeDtypeStruct(image.shape, BF16),
            jax.ShapeDtypeStruct(weight.shape, F32),
            jax.ShapeDtypeStruct((1, channels), F32),
        ),
        in_specs=[vmem] * 3,
        out_specs=(hbm, hbm, hbm, hbm),
        scratch_shapes=[
            pltpu.VMEM(weight.shape, F32),
            pltpu.VMEM((1, channels), F32),
            pltpu.SemaphoreType.DMA((4,)),
        ],
        compiler_params=pltpu.CompilerParams(vmem_limit_bytes=8 * 2**20),
    )(act_c, grad_c, total)
    return act, grad, gw, gb.reshape(channels)


def solution(mesh):
    return jax.shard_map(
        shards,
        mesh=mesh,
        in_specs=(P(None, "row", "col"), P(), P(), P(None, "row", "col")),
        out_specs=(P(None, "row", "col"), P(None, "row", "col"), P(), P()),
        check_vma=False,
    )
```

```python
import math

import jax
import jax.numpy as jnp
from jax import lax
from jax.experimental import pallas as pl
from jax.experimental.pallas import tpu as pltpu
from jax.sharding import PartitionSpec as P

MESH = pl.DeviceIdType.MESH
BF16 = jnp.bfloat16
F32 = jnp.float32
DIL = 16
LANES = 128
PLANE = 32
DEPTH = 16
COEF = 0.7978845608
CUBIC = 0.044715


def ring_order(count):
    return sorted(range(1, count), key=lambda k: -min(k, count - k))


def gelu_pair(z):
    square = z * z
    t = jnp.tanh(z * (COEF + (COEF * CUBIC) * square))
    half = 0.5 + 0.5 * t
    bend = (1.0 - t * t) * (0.5 * COEF + (1.5 * COEF * CUBIC) * square)
    return z * half, half + z * bend


def lanes_of(row, count=1):
    return slice(row * LANES, (row + count) * LANES)


def body(
    rows, scale,
    image, weight_in, bias_in, cotangent,
    act_c, grad_c, total,
    weight, bias, xin, cin, cot, stack, gstack, xside, gleft, gright,
    cot_s, act_s, grad_s, act, accs,
    terms, gathered, layers, piece,
    local_sem, xsend, xrecv, gsend, grecv, rsend, rrecv, chain_a, chain_b, chain_c, chain_d,
):
    xleft, xright = xside.at[0], xside.at[1]
    cot_l, cot_r = cot_s.at[0], cot_s.at[1]
    act_l, act_r = act_s.at[0], act_s.at[1]
    grad_l, grad_r = grad_s.at[0], grad_s.at[1]
    channels = image.shape[0]
    ext = rows + 2 * DIL
    groups = rows // 8
    row = lax.axis_index("row")
    col = lax.axis_index("col")
    nrow, ncol = lax.axis_size("row"), lax.axis_size("col")
    z = row % DEPTH
    y = (col // 8) * 2 + row // DEPTH
    x = (col // 2) % 4
    core = col % 2
    me = (row // DEPTH) * 16 + col

    def at(drow, dcol):
        return {"row": (row + drow + nrow) % nrow, "col": (col + dcol + ncol) % ncol}

    def deep(k):
        return {"row": (row // DEPTH) * DEPTH + (z + k + DEPTH) % DEPTH, "col": col}

    hops = lambda d: min(d, 4 - d)
    offsets = [(dy, dx, dc) for dy in range(4) for dx in range(4) for dc in range(2)][1:]
    offsets = sorted(offsets, key=lambda o: -(hops(o[0]) + hops(o[1])))
    plane = []
    for dy, dx, dc in offsets:
        py, px, pc = (y + dy) % 4, (x + dx) % 4, (core + dc) % 2
        pcol = (py // 2) * 8 + px * 2 + pc
        plane.append(({"row": (py % 2) * DEPTH + z, "col": pcol}, (py % 2) * 16 + pcol))

    barrier = pltpu.get_barrier_semaphore()
    beside = [at(-1, 0), at(1, 0)]
    greeted = [at(0, -1), at(0, 1)] + beside
    greeted += [deep(k) for k in (1, -1)]
    greeted += [peer for (peer, _), o in zip(plane, offsets) if hops(o[0]) + hops(o[1]) <= 1]
    for peer in greeted:
        pl.semaphore_signal(barrier, inc=1, device_id=peer, device_id_type=MESH)

    load_x = pltpu.make_async_copy(image, xin.at[:, DIL : DIL + rows, :], local_sem.at[0])
    load_c = pltpu.make_async_copy(cotangent, cin, local_sem.at[1])
    load_w = pltpu.make_async_copy(weight_in, weight, local_sem.at[2])
    load_b = pltpu.make_async_copy(bias_in, bias, local_sem.at[3])
    for load in (load_x, load_w, load_b, load_c):
        load.start()

    lane = lax.broadcasted_iota(jnp.int32, (channels, LANES), 1)
    slot = lane // DIL
    top, bottom = row == 0, row == nrow - 1
    first, last = col == 0, col == ncol - 1
    has = {
        "u": row > 0, "d": row < nrow - 1, "l": col > 0, "r": col < ncol - 1,
        "ul": (row > 0) & (col > 0), "ur": (row > 0) & (col < ncol - 1),
        "dl": (row < nrow - 1) & (col > 0), "dr": (row < nrow - 1) & (col < ncol - 1),
    }
    step = {
        "u0": (-1, 0), "d0": (1, 0), "u1": (-1, 0), "d1": (1, 0), "l": (0, -1), "r": (0, 1),
        "ul": (-1, -1), "ur": (-1, 1), "dl": (1, -1), "dr": (1, 1),
    }
    mirror = {
        "u0": "d0", "d0": "u0", "u1": "d1", "d1": "u1", "l": "r", "r": "l",
        "ul": "dr", "dr": "ul", "ur": "dl", "dl": "ur",
    }
    for n in ("u0", "u1", "d0", "d1"):
        has[n] = has[n[0]]
    names = list(step)
    vertical = ["d0", "u0", "d1", "u1"]
    sideways = ["l", "r", "ul", "ur", "dl", "dr"]

    low, center, high = (slice(k * channels, (k + 1) * channels) for k in range(3))
    above, below = lanes_of(0, 2), lanes_of(2 + groups, 2)
    level = lanes_of(2, groups)

    def halo_copies(top_src, bottom_src, top_dst, bottom_dst, own_l, own_r, left, right, send, recv):
        src_dst = {
            "u0": (top_src(0), bottom_dst(0)),
            "u1": (top_src(1), bottom_dst(1)),
            "d0": (bottom_src(0), top_dst(0)),
            "d1": (bottom_src(1), top_dst(1)),
            "l": (own_l(0, groups), right.at[:, level]),
            "r": (own_r(0, groups), left.at[:, level]),
            "ul": (own_l(0, 2), right.at[:, below]),
            "ur": (own_r(0, 2), left.at[:, below]),
            "dl": (own_l(groups - 2, 2), right.at[:, above]),
            "dr": (own_r(groups - 2, 2), left.at[:, above]),
        }
        return {
            n: pltpu.make_async_remote_copy(
                src, dst, send.at[names.index(n)], recv.at[names.index(n)],
                device_id=at(*step[n]), device_id_type=MESH,
            )
            for n, (src, dst) in src_dst.items()
        }

    def when_each(directions, predicate, action):
        for n in directions:
            pl.when(predicate(n))(lambda n=n: action(n))

    def send(copies, directions):
        when_each(directions, lambda n: has[n], lambda n: copies[n].start())

    def await_from(copies, directions):
        when_each(directions, lambda n: has[n], lambda n: copies[mirror[n]].wait_recv())

    def await_sent(copies):
        when_each(names, lambda n: has[n], lambda n: copies[n].wait_send())

    def clear(ref):
        ref[...] = jnp.zeros(ref.shape, ref.dtype)

    def zero_edges(left, right, top_dst, bottom_dst):
        pl.when(first)(lambda: clear(left))
        pl.when(last)(lambda: clear(right))

        @pl.when(top)
        def _():
            clear(top_dst)
            clear(left.at[:, above])
            clear(right.at[:, above])

        @pl.when(bottom)
        def _():
            clear(bottom_dst)
            clear(left.at[:, below])
            clear(right.at[:, below])

    def pack(source, part, r, column, target, to, g):
        merged = None
        for k in range(8):
            v = source[part, lanes_of(r + k)]
            turn = (DIL * k - column) % LANES
            v = pltpu.roll(v, turn, 1) if turn else v
            merged = v if merged is None else jnp.where(slot == k, v, merged)
        target[to, lanes_of(g)] = merged

    def unpack(target, part, r, left, right, g, k):
        a, b = left[:, lanes_of(g)], right[:, lanes_of(g)]
        a = pltpu.roll(a, LANES - DIL * k, 1) if k else a
        b = pltpu.roll(b, LANES - DIL - DIL * k, 1) if k < 7 else b
        v = target[part, lanes_of(r)]
        target[part, lanes_of(r)] = jnp.where(lane < DIL, a, jnp.where(lane >= LANES - DIL, b, v))

    def shift_row(source, r):
        v = source[center, lanes_of(r)]
        source[low, lanes_of(r)] = pltpu.roll(v, DIL, 1)
        source[high, lanes_of(r)] = pltpu.roll(v, LANES - DIL, 1)

    def merge_group(source, left, right, g):
        lv, rv = left[:, lanes_of(g)], right[:, lanes_of(g)]
        for k in range(8):
            r = lanes_of(8 * g + k)
            a = lv if k == 0 else pltpu.roll(lv, LANES - DIL * k, 1)
            b = rv if k == 7 else pltpu.roll(rv, LANES - DIL - DIL * k, 1)
            source[low, r] = jnp.where(lane < DIL, a, source[low, r])
            source[high, r] = jnp.where(lane >= LANES - DIL, b, source[high, r])

    def transpose_in(src, src_row, dst, part, dst_row, count=DIL):
        v = jnp.transpose(src[:, src_row : src_row + count, :], (1, 0, 2))
        for h in range(count):
            dst[part, lanes_of(dst_row + h)] = v[h]

    def transpose_out(value, dst, dst_row):
        v = jnp.stack([value[:, lanes_of(h)] for h in range(DIL)], axis=0)
        dst[:, dst_row : dst_row + DIL, :] = jnp.transpose(v, (1, 0, 2))

    bias_sum = [jnp.zeros((channels, LANES), F32)]

    def pixels(source, offsets, count, factor):
        z_val = offset
        for a in range(3):
            z_val = z_val + jnp.dot(
                forward[a], source[:, lanes_of(offsets[a], count)], preferred_element_type=F32
            )
        value, slope = gelu_pair(z_val)
        g = (factor.astype(F32) * slope).astype(BF16)
        wide = g.astype(F32)
        part = bias_sum[0]
        for h in range(count):
            part = part + wide[:, lanes_of(h)]
        bias_sum[0] = part
        return value.astype(BF16), g

    def forward_rows(r0, count):
        for r in range(r0, r0 + count, 4):
            value, g = pixels(stack, [r + DIL * a for a in range(3)], 4, cot[:, lanes_of(r, 4)])
            act[:, lanes_of(r, 4)] = value
            gstack[center, lanes_of(r + DIL, 4)] = g

    early, late = 1 - core, core

    def forward_edges(side, g0, count):
        source, factor = xside.at[side], cot_s.at[side]
        for g in range(g0, g0 + count, 2):
            value, grad = pixels(source, [g + 2 * a for a in range(3)], 2, factor[:, lanes_of(g, 2)])
            act_s[side, :, lanes_of(g, 2)] = value
            grad_s[side, :, lanes_of(g, 2)] = grad

    def pixel_sum(left, right):
        return lax.dot_general(left, right, (((1,), (1,)), ((), ())), preferred_element_type=F32)

    def weight_rows(h0, count):
        for a in range(3):
            inner[a] = inner[a] + pixel_sum(
                gstack[center, lanes_of(DIL + h0, count)], stack[:, lanes_of(h0 + DIL * a, count)]
            )

    def weight_edges(side, g0, count):
        for a in range(3):
            inner[a] = inner[a] + pixel_sum(
                grad_s[side, :, lanes_of(g0, count)], xside[side, :, lanes_of(g0 + 2 * a, count)]
            )

    def rows_of(ref, r0):
        return lambda k: ref.at[:, r0 + 8 * k : r0 + 8 * k + 8, :]

    def lines_of(r0):
        return lambda k: gstack.at[center, lanes_of(r0 + 8 * k, 8)]

    load_x.wait()
    for h in range(0, rows, DIL):
        transpose_in(xin, DIL + h, stack, center, DIL + h)
    for g in range(groups):
        pack(stack, center, DIL + 8 * g, 0, xleft, center, 2 + g)
        pack(stack, center, DIL + 8 * g, LANES - DIL, xright, center, 2 + g)

    pl.semaphore_wait(barrier, len(greeted))
    xcopies = halo_copies(
        rows_of(image, 0), rows_of(image, rows - DIL), rows_of(xin, 0), rows_of(xin, rows + DIL),
        lambda g, n: xleft.at[center, lanes_of(2 + g, n)],
        lambda g, n: xright.at[center, lanes_of(2 + g, n)],
        xleft.at[low], xright.at[high], xsend, xrecv,
    )
    adjacent = [peer for (peer, _), o in zip(plane, offsets) if hops(o[0]) + hops(o[1]) == 1 and o[2] == 0]
    adjacent += [deep(1), deep(-1)]
    for peer in adjacent:
        pl.semaphore_signal(chain_d, inc=1, device_id=peer, device_id_type=MESH)
    for peer in beside:
        pl.semaphore_signal(chain_c, inc=1, device_id=peer, device_id_type=MESH)
    send(xcopies, sideways[:2] + vertical)
    zero_edges(
        xleft.at[low], xright.at[high], xin.at[:, 0:DIL, :], xin.at[:, rows + DIL : ext, :]
    )
    for h in range(rows):
        shift_row(stack, DIL + h)
    pl.semaphore_wait(chain_c, len(beside))
    pl.semaphore_wait(chain_d, len(adjacent))
    chain = [peer for (peer, _), o in zip(plane, offsets) if o[0] % 2 and o[1] % 2 and o[2] == 0]
    chain += [deep(2), deep(-2)]
    for peer in chain:
        pl.semaphore_signal(chain_a, inc=1, device_id=peer, device_id_type=MESH)
    send(xcopies, sideways[2:])
    load_c.wait()
    for h in range(0, rows, DIL):
        transpose_in(cin, h, cot, slice(0, channels), h)
    for g in range(groups):
        pack(cot, slice(0, channels), 8 * g, 0, cot_l, slice(0, channels), g)
        pack(cot, slice(0, channels), 8 * g, LANES - DIL, cot_r, slice(0, channels), g)
    inside = (lane >= DIL) & (lane < LANES - DIL)
    for h in range(rows):
        v = cot[:, lanes_of(h)]
        cot[:, lanes_of(h)] = jnp.where(inside, v, jnp.zeros_like(v))
    load_w.wait()
    load_b.wait()
    forward = [
        jnp.concatenate([weight[a, e] for e in range(3)], axis=1) for a in range(3)
    ]
    backward = [
        jnp.concatenate([weight[2 - a, 2 - e].T for e in range(3)], axis=1) for a in range(3)
    ]
    sub = lax.broadcasted_iota(jnp.int32, (channels, channels), 0)
    lan = lax.broadcasted_iota(jnp.int32, (channels, channels), 1)
    offset = jnp.sum(jnp.where(sub == lan, bias[...], 0.0), axis=1, keepdims=True)
    accs[...] = jnp.zeros_like(accs)


    forward_rows(DIL, rows - 2 * DIL)
    blocks = [gstack[center, lanes_of(DIL + h, DIL)] for h in range(DIL, rows - DIL, DIL)]
    none = jnp.zeros_like(blocks[0])
    stacked = None
    for k in range(len(blocks) + 2):
        lines = [blocks[k - a] if 0 <= k - a < len(blocks) else none for a in range(3)]
        d = lax.dot_general(
            jnp.concatenate(lines, axis=0),
            stack[:, lanes_of((k + 1) * DIL, DIL)],
            (((1,), (1,)), ((), ())),
            preferred_element_type=F32,
        )
        stacked = d if stacked is None else stacked + d
    inner = [stacked[a * channels : (a + 1) * channels] for a in range(3)]

    for g in range(groups):
        pack(stack, center, DIL + 8 * g, DIL, xleft, high, 2 + g)
        pack(stack, center, DIL + 8 * g, LANES - 2 * DIL, xright, low, 2 + g)

    def rim(k):
        await_from(xcopies, [f"u{k}", f"d{k}"])
        for base, g in ((8 * k, k), (rows + DIL + 8 * k, 2 + groups + k)):
            transpose_in(xin, base, stack, center, base, 8)
            for h in range(8):
                shift_row(stack, base + h)
        for r in (8 * k, rows - DIL + 8 * k):
            forward_rows(r, 8)
            weight_rows(r, 8)
        for base, g in ((8 * k, k), (rows + DIL + 8 * k, 2 + groups + k)):
            pack(stack, center, base, 0, xleft, center, g)
            pack(stack, center, base, DIL, xleft, high, g)
            pack(stack, center, base, LANES - 2 * DIL, xright, low, g)
            pack(stack, center, base, LANES - DIL, xright, center, g)

    def await_side(right):
        pl.when(right & has["r"])(lambda: xcopies[mirror["r"]].wait_recv())
        pl.when(jnp.logical_not(right) & has["l"])(lambda: xcopies[mirror["l"]].wait_recv())

    rim(0)
    await_side(early == 1)
    forward_edges(early, 2, groups - 4)
    weight_edges(early, 2, groups - 4)
    rim(1)
    await_side(late == 1)
    forward_edges(late, 2, groups - 4)
    weight_edges(late, 2, groups - 4)
    await_from(xcopies, ["ul", "ur", "dl", "dr"])
    for side in (0, 1):
        for g in (0, groups - 2):
            forward_edges(side, g, 2)
            weight_edges(side, g, 2)
    for a in range(3):
        accs[a, :, 0 : 3 * channels] = inner[a]
    accs[0, :, 3 * channels : 3 * channels + 1] = jnp.sum(bias_sum[0], axis=1, keepdims=True)
    for a in range(3):
        terms[:, 0, lanes_of(a)] = accs[a]
    pl.semaphore_wait(chain_a, len(chain))
    for k in (4, -4):
        pl.semaphore_signal(chain_b, inc=1, device_id=deep(k), device_id_type=MESH)

    def remote(src, dst, k, peer):
        pltpu.make_async_remote_copy(
            src, dst, rsend.at[k], rrecv.at[k], device_id=peer, device_id_type=MESH
        ).start()

    def drain(sem, buffer):
        pltpu.make_async_copy(buffer, buffer, sem).wait()

    for peer, index in plane:
        remote(terms.at[index], gathered.at[me], 0, peer)
    gathered[me] = terms[me]

    gcopies = halo_copies(
        lines_of(DIL), lines_of(rows), lines_of(0), lines_of(rows + DIL),
        lambda g, n: grad_l.at[:, lanes_of(g, n)],
        lambda g, n: grad_r.at[:, lanes_of(g, n)],
        gleft, gright, gsend, grecv,
    )
    send(gcopies, sideways)
    rim_first = [r for r in range(rows) if r < DIL or r >= rows - DIL]
    rim_first += [r for r in range(DIL, rows - DIL)]
    for n, r in enumerate(rim_first):
        unpack(gstack, center, DIL + r, grad_l, grad_r, r // 8, r % 8)
        if n == 2 * DIL - 1:
            send(gcopies, vertical)
    for r in range(rows):
        unpack(act, slice(0, channels), r, act_l, act_r, r // 8, r % 8)
    zero_edges(
        gleft, gright,
        gstack.at[center, lanes_of(0, DIL)], gstack.at[center, lanes_of(rows + DIL, DIL)],
    )
    for h in range(0, rows, DIL):
        transpose_out(act[:, lanes_of(h, DIL)], act_c, h)
    for h in range(rows):
        shift_row(gstack, DIL + h)
    pl.semaphore_wait(chain_b, 2)

    drain(rrecv.at[0], gathered.at[pl.ds(0, PLANE - 1)])
    piece[0] = jnp.sum(gathered[...], axis=0)
    for k in ring_order(DEPTH):
        remote(piece.at[0], layers.at[z], 1, deep(k))
    layers[z] = piece[0]

    await_from(gcopies, names)
    for base in (0, rows + DIL):
        for h in range(DIL):
            shift_row(gstack, base + h)
    for g in range(4 + groups):
        merge_group(gstack, gleft, gright, g)
    for h in range(0, rows, DIL):
        tiles = []
        for r in (h, h + 8):
            out = None
            for a in range(3):
                d = jnp.dot(
                    backward[a], gstack[:, lanes_of(r + DIL * a, 8)], preferred_element_type=F32
                )
                out = d if out is None else out + d
            tiles.append(out.astype(BF16))
        transpose_out(jnp.concatenate(tiles, axis=1), grad_c, h)

    drain(rrecv.at[1], layers.at[pl.ds(0, DEPTH - 1)])
    piece[1] = jnp.sum(layers[...], axis=0) * scale
    for peer, index in plane:
        remote(piece.at[1], total.at[me], 2, peer)
    total[me] = piece[1]
    await_sent(xcopies)
    await_sent(gcopies)
    drain(rsend.at[0], gathered.at[pl.ds(0, PLANE - 1)])
    drain(rsend.at[1], layers.at[pl.ds(0, DEPTH - 1)])
    drain(rrecv.at[2], total.at[pl.ds(0, PLANE - 1)])
    drain(rsend.at[2], total.at[pl.ds(0, PLANE - 1)])


def write_out(act_c, grad_c, total, act_out, grad_out, gw_out, gb_out, gw, gb, sem):
    channels = act_c.shape[0]
    copies = [
        pltpu.make_async_copy(act_c, act_out, sem.at[0]),
        pltpu.make_async_copy(grad_c, grad_out, sem.at[1]),
        pltpu.make_async_copy(gw, gw_out, sem.at[2]),
        pltpu.make_async_copy(gb, gb_out, sem.at[3]),
    ]
    copies[0].start()
    copies[1].start()
    sub = lax.broadcasted_iota(jnp.int32, (channels, channels), 0)
    lan = lax.broadcasted_iota(jnp.int32, (channels, channels), 1)
    for a in range(3):
        tile = total[:, 0, lanes_of(a)]
        for e in range(3):
            gw[a, e] = tile[:, e * channels : (e + 1) * channels]
        if a == 0:
            column = tile[:, 3 * channels : 3 * channels + 1]
            gb[...] = jnp.sum(jnp.where(sub == lan, column, 0.0), axis=0, keepdims=True)
    copies[2].start()
    copies[3].start()
    for copy in copies:
        copy.wait()


def shards(image, weight, bias, cotangent):
    channels, rows, columns = image.shape
    assert columns == LANES and rows % DIL == 0 and channels == PLANE
    count = rows * lax.axis_size("row") * columns * lax.axis_size("col")
    scale = 1.0 / math.sqrt(count)
    ext = rows + 2 * DIL
    groups = rows // 8
    vmem = pl.BlockSpec(memory_space=pltpu.VMEM)
    hbm = pl.BlockSpec(memory_space=pltpu.HBM)
    taps = pltpu.VMEM((2, 3 * channels, (groups + 4) * LANES), BF16)
    rim = pltpu.VMEM((channels, (groups + 4) * LANES), BF16)
    edge = pltpu.VMEM((2, channels, groups * LANES), BF16)
    tile = pltpu.VMEM((channels, rows, LANES), BF16)
    line = (1, 3 * LANES)

    def kernel(*refs):
        body(rows, scale, *refs)

    act_c, grad_c, total = pl.pallas_call(
        kernel,
        out_shape=(
            jax.ShapeDtypeStruct(image.shape, BF16),
            jax.ShapeDtypeStruct(image.shape, BF16),
            jax.ShapeDtypeStruct((PLANE,) + line, F32),
        ),
        in_specs=[hbm] * 4,
        out_specs=(vmem, vmem, vmem),
        scratch_shapes=[
            pltpu.VMEM(weight.shape, BF16),
            pltpu.VMEM((1, channels), F32),
            pltpu.VMEM((channels, ext, LANES), BF16),
            tile,
            pltpu.VMEM((channels, rows * LANES), BF16),
            pltpu.VMEM((3 * channels, ext * LANES), BF16),
            pltpu.VMEM((3 * channels, ext * LANES), BF16),
            taps, rim, rim, edge, edge, edge,
            pltpu.VMEM((channels, rows * LANES), BF16),
            pltpu.VMEM((3, channels, LANES), F32),
            pltpu.VMEM((PLANE,) + line, F32),
            pltpu.VMEM((PLANE,) + line, F32),
            pltpu.VMEM((DEPTH,) + line, F32),
            pltpu.VMEM((2,) + line, F32),
            pltpu.SemaphoreType.DMA((4,)),
            pltpu.SemaphoreType.DMA((10,)),
            pltpu.SemaphoreType.DMA((10,)),
            pltpu.SemaphoreType.DMA((10,)),
            pltpu.SemaphoreType.DMA((10,)),
            pltpu.SemaphoreType.DMA((3,)),
            pltpu.SemaphoreType.DMA((3,)),
            pltpu.SemaphoreType.REGULAR,
            pltpu.SemaphoreType.REGULAR,
            pltpu.SemaphoreType.REGULAR,
            pltpu.SemaphoreType.REGULAR,
        ],
        compiler_params=pltpu.CompilerParams(
            collective_id=0, has_side_effects=True, vmem_limit_bytes=20 * 2**20
        ),
    )(*(pltpu.with_memory_space_constraint(v, pltpu.HBM) for v in (image, weight, bias.reshape(1, channels), cotangent)))
    act, grad, gw, gb = pl.pallas_call(
        write_out,
        out_shape=(
            jax.ShapeDtypeStruct(image.shape, BF16),
            jax.ShapeDtypeStruct(image.shape, BF16),
            jax.ShapeDtypeStruct(weight.shape, F32),
            jax.ShapeDtypeStruct((1, channels), F32),
        ),
        in_specs=[vmem] * 3,
        out_specs=(hbm, hbm, hbm, hbm),
        scratch_shapes=[
            pltpu.VMEM(weight.shape, F32),
            pltpu.VMEM((1, channels), F32),
            pltpu.SemaphoreType.DMA((4,)),
        ],
        compiler_params=pltpu.CompilerParams(vmem_limit_bytes=8 * 2**20),
    )(act_c, grad_c, total)
    return act, grad, gw, gb.reshape(channels)


def solution(mesh):
    return jax.shard_map(
        shards,
        mesh=mesh,
        in_specs=(P(None, "row", "col"), P(), P(), P(None, "row", "col")),
        out_specs=(P(None, "row", "col"), P(None, "row", "col"), P(), P()),
        check_vma=False,
    )
```
